256 devices in a mesh: dp: 2 (over core), expert: 4 (over x), tensor: 32 (over z, y).
Axes of the slice: x: 4, y: 4, z: 8, core: 2. Of those that a mesh axis runs over, the one named last changes fastest.
Arguments:
- tokens: bfloat16 [1024, 3072], P(('dp', 'expert')), may hold values from -6 to 6
- cotangent: bfloat16 [1024, 3072], P(('dp', 'expert')), may hold values from -6 to 6
- gate_weights: bfloat16 [1024, 2], P(('dp', 'expert')), may hold values from 0.099609375 to 0.8984375
- expert_ids: int32 [1024, 2], P(('dp', 'expert')), may hold values from 0 to 3, all different within a row; in each aligned block of 128 rows (0 to 127, 128 to 255, ...) at most 96 rows name the same one
- w_gate: bfloat16 [4, 3072, 8192], P('expert', 'dp', 'tensor'), may hold values from -0.109375 to 0.109375
- w_up: bfloat16 [4, 3072, 8192], P('expert', 'dp', 'tensor'), may hold values from -0.109375 to 0.109375
- w_down: bfloat16 [4, 3072, 8192], P('expert', 'dp', 'tensor'), may hold values from -0.0625 to 0.0625
Outputs:
- input_grad: bfloat16 [1024, 3072], P(('dp', 'expert'))
- gate_grad: bfloat16 [1024, 2], P(('dp', 'expert'))
- grad_gate: bfloat16 [4, 3072, 8192], P('expert', 'dp', 'tensor')
- grad_up: bfloat16 [4, 3072, 8192], P('expert', 'dp', 'tensor')
- grad_down: bfloat16 [4, 3072, 8192], P('expert', 'dp', 'tensor')
The draws below stay inside these ranges and needn't reach their ends.
Inputs may be any that keep to these rules, and one draw needn't show every extreme that they name: `expert_ids`: each token names 2 different experts. Among the 128 tokens of one block, no expert is named more than 96 times, and in some blocks one expert is named exactly 96 times.
All inputs are finite; a program needn't handle non-finite values.
Results may differ from the reference program's by a relative error of at most 0.025.
Values may be sent and summed in bfloat16 or wider, within the bound.
No kernel may reach another device: no remote copies, remote signals or barrier semaphores. Data moves between devices by JAX's collectives and lax.ppermute only.
A program may use at most 64 MiB of HBM per device.

```python
import math
import jax
import jax.numpy as jnp
import numpy as np
from jax import lax

D = 3072
FF = 8192
TOP = 2
TOK_DEV = 128
EXPERTS = 4
CAP = 96
TOKENS = 1024
N_DP = 2
N_EXPERT = 4
N_TENSOR = 32


def block_scale(rng, dims, shards, low, high):
    gain, own = 1.0, jax.random.fold_in(rng, 6)
    for dim, shards_of in shards:
        steps = jnp.exp(jax.random.uniform(jax.random.fold_in(own, dim), (shards_of,), jnp.float32, low / len(shards), high / len(shards)))
        gain = gain * jnp.repeat(steps, dims[dim] // shards_of).reshape([-1 if axis == dim else 1 for axis in range(len(dims))])
    return gain


def deal_out(rng, own, number, rows, number_of, top, limit, skew):
    ranking = jax.random.permutation(rng, number_of)
    packed, common = load_shares(number_of, rows * top, limit, skew, True), load_shares(number_of, rows * top, limit, skew, False)
    places = jnp.arange(number_of)

    def named(tallies, offset_by):
        used = int((tallies > 0).sum())
        fixed = max(1, used // 4)
        shifted = fixed + (places - fixed + offset_by * (used - fixed)) % max(1, number_of - fixed)
        return jnp.zeros((number_of,), jnp.int32).at[ranking[jnp.where(places < fixed, places, shifted)]].set(jnp.asarray(tallies, jnp.int32))

    tallies = jnp.where(number % 4 == 0, named(packed, number // 4), named(common, number - number // 4 - 1))
    mixed = jax.random.permutation(jax.random.fold_in(own, 3), number_of)
    source_of, sink = mixed[0:number_of // 2 * 2:2], mixed[1:number_of // 2 * 2:2]
    margin = jnp.minimum(tallies[source_of] - 1, limit - tallies[sink]) // 2
    margin = jnp.where((source_of == ranking[0]) | (sink == ranking[0]) | (tallies[sink] == 0), 0, jnp.maximum(margin, 0))
    shifted = jax.random.randint(jax.random.fold_in(own, 4), (number_of // 2,), 0, 1 << 20) % (margin + 1)
    tallies = tallies.at[source_of].add(-shifted).at[sink].add(shifted)
    items = jnp.searchsorted(jnp.cumsum(tallies), jnp.arange(rows * top), side="right").astype(jnp.int32)
    listing = items.reshape(top, rows).T
    listing = listing[jax.random.permutation(jax.random.fold_in(own, 1), rows)]
    offset_by = jax.random.randint(jax.random.fold_in(own, 2), (rows, 1), 0, top)
    return jnp.take_along_axis(listing, (jnp.arange(top)[None, :] + offset_by) % top, axis=1)


def load_shares(count, total, limit, slope, full):
    loads = [(1 << 20) // math.isqrt(grade ** slope) + 1 for grade in range(1, count + 1)]
    largest = limit if full else min(limit, max(-(-total // count), total * loads[0] // sum(loads)))
    least = 1 if total - largest >= count - 1 else 0
    holding, spare = [largest] + [least] * (count - 1), total - largest - least * (count - 1)
    while spare > 0:
        candidates = [i for i in range(1, count) if holding[i] < largest] or [i for i in range(1, count) if holding[i] < limit]
        mass, left = sum([loads[i] for i in candidates]), spare
        for i in candidates:
            more = min(limit - holding[i], max(1, left * loads[i] // mass), spare)
            holding[i] = holding[i] + more
            spare = spare - more
    return np.array(holding)


def gaussian(own_key, extent, scale, bound, cuts=(), kind=jnp.bfloat16):
    result = scale * jax.random.normal(own_key, extent, jnp.float32)
    if cuts:
        result = result * block_scale(own_key, extent, cuts, -0.22, 0.18)
    return jnp.clip(result, -bound, bound).astype(kind)


def setup_inputs(seed: int = 0) -> dict:
    streams_of = jax.random.split(jax.random.key(seed), 8)
    tokens = gaussian(streams_of[0], (TOKENS, D), 1.0, 6.0, ((0, 8),))
    cotangent = gaussian(streams_of[1], (TOKENS, D), 1.0, 6.0, ((0, 8),))
    gate_weights = jnp.clip(0.099609375 + 0.7988281 * jax.random.uniform(streams_of[2], (TOKENS, TOP), jnp.float32) ** block_scale(streams_of[2], (TOKENS, TOP), ((0, 8),), -0.2, 0.2), 0.099609375, 0.8984375).astype(jnp.bfloat16)
    expert_ids_keys = jax.random.split(jax.random.fold_in(streams_of[3], 1), TOKENS // TOK_DEV)
    expert_ids_turns = jax.random.permutation(jax.random.fold_in(streams_of[3], 3), TOKENS // TOK_DEV)
    expert_ids = jax.vmap(lambda own, number: deal_out(jax.random.fold_in(streams_of[3], 2), own, number, TOK_DEV, EXPERTS, TOP, CAP, 2))(expert_ids_keys, expert_ids_turns).reshape((TOKENS, TOP))
    w_gate = gaussian(streams_of[4], (EXPERTS, D, FF), D ** -0.5, 0.109375, ((0, 4), (1, 2), (2, 32)))
    w_up = gaussian(streams_of[5], (EXPERTS, D, FF), D ** -0.5, 0.109375, ((0, 4), (1, 2), (2, 32)))
    w_down = gaussian(streams_of[6], (EXPERTS, D, FF), FF ** -0.5, 0.0625, ((0, 4), (1, 2), (2, 32)))
    return dict(tokens=tokens, cotangent=cotangent, gate_weights=gate_weights, expert_ids=expert_ids, w_gate=w_gate, w_up=w_up, w_down=w_down)


def slot_numbers(expert_ids, experts):
    labels = lax.broadcasted_iota(jnp.int32, (1, 1, experts), 2)
    onehot = (expert_ids[:, :, None] == labels).astype(jnp.int32).reshape(-1, experts)
    earlier = jnp.cumsum(onehot, axis=0) - onehot
    return jnp.sum(earlier * onehot, axis=1).astype(jnp.int32)


def entry_table(expert_ids, experts, capacity):
    flat_slot = slot_numbers(expert_ids, experts)
    target = expert_ids.reshape(-1).astype(jnp.int32) * capacity + flat_slot
    entry_count = expert_ids.shape[0] * expert_ids.shape[1]
    entries = jnp.full((experts * capacity,), entry_count, jnp.int32)
    entries = entries.at[target].set(jnp.arange(entry_count, dtype=jnp.int32))
    return target, entries


def fill_buffers(tokens, cotangent, gate_weights, entries):
    model_width = tokens.shape[1]
    zero_row = jnp.zeros((1, model_width), tokens.dtype)
    token_rows = (entries // 2).astype(jnp.int32)
    token_pad = jnp.concatenate([tokens, zero_row], 0)
    grad_pad = jnp.concatenate([cotangent, zero_row], 0)
    weight_pad = jnp.concatenate([gate_weights.reshape(-1), jnp.zeros((2,), gate_weights.dtype)], 0)
    return token_pad[token_rows], grad_pad[token_rows], weight_pad[entries]


def split_units(array):
    width = array.shape[1] // N_TENSOR
    return jnp.moveaxis(array.reshape(array.shape[0], N_TENSOR, width), 1, 0)


def reference(tokens, cotangent, gate_weights, expert_ids, w_gate, w_up, w_down):
    blocks = N_DP * N_EXPERT
    x_blocks = tokens.reshape(blocks, TOK_DEV, D)
    dy_blocks = cotangent.reshape(blocks, TOK_DEV, D)
    g_blocks = gate_weights.reshape(blocks, TOK_DEV, TOP)
    id_blocks = expert_ids.reshape(blocks, TOK_DEV, TOP)

    def table_of(block_ids):
        return entry_table(block_ids, EXPERTS, CAP)

    targets, entries = jax.vmap(table_of)(id_blocks)
    x_buf, dy_buf, g_buf = jax.vmap(fill_buffers)(x_blocks, dy_blocks, g_blocks, entries)

    def by_expert(buffer, columns):
        shaped = buffer.reshape((blocks, EXPERTS, CAP) + columns)
        moved = jnp.moveaxis(shaped, 1, 0)
        return moved.reshape((EXPERTS, blocks * CAP) + columns)

    x_rows = by_expert(x_buf, (D,))
    dy_rows = by_expert(dy_buf, (D,))
    g_rows = by_expert(g_buf, ())
    half_rows = N_EXPERT * CAP
    inner = (((1,), (1,)), ((), ()))
    outer = (((0,), (0,)), ((), ()))

    def dp_total(left, right):
        total = jnp.zeros((left.shape[1], right.shape[1]), jnp.float32)
        for member in range(N_DP):
            piece = lax.dot_general(left[member * half_rows:(member + 1) * half_rows],
                                    right[member * half_rows:(member + 1) * half_rows],
                                    outer, preferred_element_type=jnp.float32).astype(jnp.bfloat16)
            piece = lax.optimization_barrier(piece)
            total = total + piece.astype(jnp.float32)
        return total.astype(jnp.bfloat16)

    def per_expert(operands):
        rows_x, rows_dy, rows_gate, gate_full, up_full, down_full = operands
        gate_pre = jnp.dot(rows_x, gate_full, preferred_element_type=jnp.float32)
        up_pre = jnp.dot(rows_x, up_full, preferred_element_type=jnp.float32)
        sigma = jax.nn.sigmoid(gate_pre)
        active = gate_pre * sigma
        hidden = (active * up_pre).astype(jnp.bfloat16)
        back = jnp.dot(rows_dy, down_full, preferred_element_type=jnp.float32)
        factor = rows_gate.astype(jnp.float32)[:, None]
        hidden_grad = factor * back
        d_pre_gate = (hidden_grad * up_pre * sigma * (1.0 + gate_pre * (1.0 - sigma))).astype(jnp.bfloat16)
        d_pre_up = (hidden_grad * active).astype(jnp.bfloat16)
        scaled = (factor * rows_dy.astype(jnp.float32)).astype(jnp.bfloat16)

        def add_sliver(carry, pieces):
            input_total, gate_total = carry
            piece_gate, piece_up, piece_hidden, piece_back, weight_gate, weight_up = pieces
            part_input = (lax.dot_general(piece_gate, weight_gate, inner, preferred_element_type=jnp.float32)
                          + lax.dot_general(piece_up, weight_up, inner, preferred_element_type=jnp.float32)).astype(jnp.bfloat16)
            part_gate = jnp.sum(piece_hidden.astype(jnp.float32) * piece_back, axis=1).astype(jnp.bfloat16)
            part_input = lax.optimization_barrier(part_input)
            part_gate = lax.optimization_barrier(part_gate)
            return (input_total + part_input.astype(jnp.float32), gate_total + part_gate.astype(jnp.float32)), None

        row_count = rows_x.shape[0]
        start = (jnp.zeros((row_count, D), jnp.float32), jnp.zeros((row_count,), jnp.float32))
        (input_sum, gate_sum), _ = lax.scan(add_sliver, start,
                                            (split_units(d_pre_gate), split_units(d_pre_up), split_units(hidden),
                                             split_units(back), split_units(gate_full), split_units(up_full)))
        slot_input = input_sum.astype(jnp.bfloat16)
        slot_gate = gate_sum.astype(jnp.bfloat16)
        return (slot_input, slot_gate, dp_total(rows_x, d_pre_gate), dp_total(rows_x, d_pre_up),
                dp_total(scaled, hidden))

    slot_input, slot_gate, grad_gate, grad_up, grad_down = lax.map(
        per_expert, (x_rows, dy_rows, g_rows, w_gate, w_up, w_down))
    slot_input = jnp.moveaxis(slot_input.reshape(EXPERTS, blocks, CAP, D), 1, 0).reshape(blocks, EXPERTS * CAP, D)
    slot_gate = jnp.moveaxis(slot_gate.reshape(EXPERTS, blocks, CAP), 1, 0).reshape(blocks, EXPERTS * CAP)

    def combine(block_input, block_gate, target):
        rows = block_input[target].reshape(TOK_DEV, TOP, D)
        summed = jnp.sum(rows.astype(jnp.float32), axis=1).astype(jnp.bfloat16)
        return summed, block_gate[target].reshape(TOK_DEV, TOP)

    input_grad, gate_grad = jax.vmap(combine)(slot_input, slot_gate, targets)
    return (input_grad.reshape(TOKENS, D), gate_grad.reshape(TOKENS, TOP), grad_gate, grad_up, grad_down)
```

```python
import functools

import jax
import jax.numpy as jnp
from jax import lax
from jax.experimental import pallas as pl
from jax.experimental.pallas import tpu as pltpu
from jax.sharding import Mesh, PartitionSpec as P


BF = jnp.bfloat16
F32 = jnp.float32
NT = (((1,), (1,)), ((), ()))
TN = (((0,), (0,)), ((), ()))
OFFSETS = (0, 1, -1, 2)
LANES = 128


def vmem(count):
    return [pl.BlockSpec(memory_space=pltpu.VMEM)] * count


def smem():
    return pl.BlockSpec(memory_space=pltpu.SMEM)


def call(kernel, outs, operands, name):
    return pl.pallas_call(
        kernel,
        out_shape=outs,
        in_specs=[smem()] + vmem(len(operands) - 1),
        out_specs=jax.tree.map(lambda _: pl.BlockSpec(memory_space=pltpu.VMEM), outs),
        name=name,
    )(*operands)


def dispatch_kernel(pos, ids_ref, gw_ref, tok_ref, cot_ref, *outs):
    tokens, width = tok_ref.shape
    slots = outs[0].shape[0]
    experts = len(outs)
    ids = ids_ref[...]
    gates = gw_ref[...].astype(F32)
    before = (
        lax.broadcasted_iota(jnp.int32, (tokens, tokens), 0)
        < lax.broadcasted_iota(jnp.int32, (tokens, tokens), 1)
    ).astype(BF)
    own = pos[1]
    wanted = [lax.rem(own + offset + experts, experts) for offset in OFFSETS]
    rows = []
    weights = []
    for expert in wanted:
        hit = ids == expert
        rows.append(jnp.max(hit.astype(F32), axis=0, keepdims=True))
        weights.append(jnp.sum(jnp.where(hit, gates, 0.0), axis=0, keepdims=True))
    member = jnp.concatenate(rows + [jnp.zeros((8 - experts, tokens), F32)], axis=0)
    rank = jnp.dot(member.astype(BF), before, preferred_element_type=F32)
    token = lax.broadcasted_iota(jnp.int32, (8, tokens), 1).astype(F32) + 1.0
    slot = lax.broadcasted_iota(jnp.int32, (slots, tokens), 0).astype(F32)
    line = lax.broadcasted_iota(jnp.int32, (8, tokens), 0)
    tok = tok_ref[...]
    cot = cot_ref[...]
    for j in range(experts):
        pick = jnp.where(
            (slot == rank[j : j + 1]) & (member[j : j + 1] > 0.5), 1.0, 0.0
        ).astype(BF)
        outs[j][:, :width] = jnp.dot(pick, tok, preferred_element_type=F32).astype(BF)
        outs[j][:, width : 2 * width] = jnp.dot(pick, cot, preferred_element_type=F32).astype(BF)
        facts = jnp.where(line == 0, weights[j], jnp.where(line == 1, token, 0.0))
        facts = jnp.concatenate([facts, jnp.zeros((LANES - 8, tokens), F32)], axis=0).astype(BF)
        outs[j][:, 2 * width :] = lax.dot_general(
            pick, facts, NT, preferred_element_type=F32
        ).astype(BF)


def expert_kernel(pos, msg_ref, wg_ref, wu_ref, wd_ref, *outs):
    parts = outs[:4]
    dpg_ref, dpu_ref, gh_ref = outs[4:]
    width = wg_ref.shape[0]
    block = width // 4
    x = msg_ref[:, :width]
    dy = msg_ref[:, width : 2 * width]
    g = msg_ref[:, 2 * width : 2 * width + 1].astype(F32)
    gate = jnp.dot(x, wg_ref[...], preferred_element_type=F32)
    up = jnp.dot(x, wu_ref[...], preferred_element_type=F32)
    back = jnp.dot(dy, wd_ref[...], preferred_element_type=F32)
    sig = jax.nn.sigmoid(gate)
    act = gate * sig
    hid = act * up
    hidden = hid.astype(BF)
    slot_gate = jnp.sum(hidden.astype(F32) * back, axis=1, keepdims=True)
    hg = g * back
    dpg = (hg * up * sig * (1.0 + gate * (1.0 - sig))).astype(BF)
    dpu = (hg * act).astype(BF)
    dpg_ref[...] = dpg
    dpu_ref[...] = dpu
    gh_ref[...] = (g * hid).astype(BF)
    lane = lax.broadcasted_iota(jnp.int32, (x.shape[0], LANES), 1)
    extra = jnp.where(lane == pos[1], slot_gate, 0.0).astype(BF)
    for j in range(4):
        at = pl.multiple_of(lax.rem(pos[3] + j, 4) * block, block)
        part = lax.dot_general(dpg, wg_ref[pl.ds(at, block), :], NT, preferred_element_type=F32)
        part += lax.dot_general(dpu, wu_ref[pl.ds(at, block), :], NT, preferred_element_type=F32)
        parts[j][:, :block] = part.astype(BF)
        parts[j][:, block:] = extra


def expand_kernel(pos, msg_ref, a_ref, b_ref, c_ref, d_ref, *outs):
    slots = a_ref.shape[0]
    rows = outs[0].shape[0]
    count = rows * len(outs)
    total = (
        a_ref[...].astype(F32) + b_ref[...].astype(F32)
        + c_ref[...].astype(F32) + d_ref[...].astype(F32)
    ).astype(BF)
    index = msg_ref[:, msg_ref.shape[1] - LANES + 1 : msg_ref.shape[1] - LANES + 2].astype(F32)
    row = lax.broadcasted_iota(jnp.int32, (slots, count), 1)
    token = lax.rem(row + pos[2] * rows, count).astype(F32) + 1.0
    pick = jnp.where(index == token, 1.0, 0.0).astype(BF)
    spread = lax.dot_general(pick, total, TN, preferred_element_type=F32).astype(BF)
    for j, out in enumerate(outs):
        out[...] = spread[j * rows : (j + 1) * rows]


def sum_kernel(pos, *refs):
    total = refs[0][...].astype(F32)
    for ref in refs[1:-1]:
        total += ref[...].astype(F32)
    refs[-1][...] = total.astype(BF)


def rows_kernel(pos, ids_ref, *refs):
    pieces, (slab_ref, gate_ref, all_ref) = refs[:-3], refs[-3:]
    rows = pieces[0].shape[0]
    width = slab_ref.shape[1]
    count = len(pieces)
    for j, piece in enumerate(pieces):
        at = pl.multiple_of(lax.rem(pos[2] - j + count, count) * rows, rows)
        slab_ref[pl.ds(at, rows), :] = piece[:, :width]
        all_ref[pl.ds(at, rows), :] = piece[:, width:].astype(F32)
    values = all_ref[...]
    lane = lax.broadcasted_iota(jnp.int32, values.shape, 1)
    ids = ids_ref[...]
    for k in range(2):
        mine = jnp.where(lane == ids[:, k : k + 1], values, 0.0)
        gate_ref[:, k : k + 1] = jnp.sum(mine, axis=1, keepdims=True).astype(BF)


def columns_kernel(pos, *refs):
    pieces, out_ref = refs[:-1], refs[-1]
    width = pieces[0].shape[1]
    for piece, shift in zip(pieces, OFFSETS):
        at = pl.multiple_of(lax.rem(pos[3] - shift + 4, 4) * width, LANES)
        out_ref[:, pl.ds(at, width)] = piece[...]


def grad_kernel(add, pos, *refs):
    xs, dys, gs, us, hs = (refs[4 * k : 4 * k + 4] for k in range(5))
    rest = refs[20:]
    def stack(group):
        return jnp.concatenate([ref[...] for ref in group], axis=0)
    x = stack(xs)
    dy = stack(dys)
    for k, (left, right) in enumerate(((x, gs), (x, us), (dy, hs))):
        total = lax.dot_general(left, stack(right), TN, preferred_element_type=F32)
        if add:
            total += rest[k][...].astype(F32)
        rest[-3 + k][...] = total.astype(BF)


def half_gradients(pos, msgs, dpgs, dpus, ghs, other, received):
    slots = msgs[0].shape[0]
    units = dpgs[0].shape[1]
    width = (msgs[0].shape[1] - LANES) // 2
    half = width // 2
    step = 256
    count = half // step

    def first(pos):
        return (1 - pos[0]) if other else pos[0]

    x_spec = pl.BlockSpec((slots, step), lambda i, pos: (0, first(pos) * count + i))
    dy_spec = pl.BlockSpec((slots, step), lambda i, pos: (0, 2 * count + first(pos) * count + i))
    d_spec = pl.BlockSpec((slots, units), lambda i, pos: (0, 0))
    o_spec = pl.BlockSpec((step, units), lambda i, pos: (i, 0))
    return pl.pallas_call(
        functools.partial(grad_kernel, received is not None),
        out_shape=[jax.ShapeDtypeStruct((half, units), BF)] * 3,
        grid_spec=pltpu.PrefetchScalarGridSpec(
            num_scalar_prefetch=1,
            grid=(count,),
            in_specs=[x_spec] * 4 + [dy_spec] * 4 + [d_spec] * 12 + [o_spec] * len(received or ()),
            out_specs=[o_spec] * 3,
        ),
        name="grad_other" if other else "grad_own",
    )(pos, *msgs, *msgs, *dpgs, *dpus, *ghs, *(received or ()))


def shift(value, axis, offset):
    size = lax.axis_size(axis)
    return lax.ppermute(value, axis, [(i, (i + offset) % size) for i in range(size)])


def shift_two(value, axes, offsets):
    a, b = lax.axis_size(axes[0]), lax.axis_size(axes[1])
    pairs = [
        (i * b + j, ((i + offsets[0]) % a) * b + (j + offsets[1]) % b)
        for i in range(a)
        for j in range(b)
    ]
    return lax.ppermute(value, axes, pairs)


def on_device(tokens, cotangent, gate_weights, expert_ids, w_gate, w_up, w_down):
    tok_count, width = tokens.shape
    slots = tok_count * 3 // 4
    units = w_gate.shape[2]
    block = width // 4
    core = lax.axis_index("dp")
    zs = lax.axis_size("z")
    rows = tok_count // zs
    pos = jnp.stack(
        [core, lax.axis_index("expert"), lax.axis_index("z"), lax.axis_index("y")]
    ).astype(jnp.int32)

    def whole(own):
        sib = shift(own, "dp", 1)
        return jnp.where(core == 0, jnp.concatenate([own, sib], 0), jnp.concatenate([sib, own], 0))

    wg, wu, wd = whole(w_gate[0]), whole(w_up[0]), whole(w_down[0])
    sent = call(
        dispatch_kernel,
        [jax.ShapeDtypeStruct((slots, 2 * width + LANES), BF)] * 4,
        (pos, expert_ids.T, gate_weights.T, tokens, cotangent),
        "dispatch",
    )
    msgs = [sent[0]] + [shift(sent[k], "expert", OFFSETS[k]) for k in (1, 2, 3)]
    dpgs, dpus, ghs, pieces = [], [], [], []
    for k, offset in enumerate(OFFSETS):
        outs = call(
            expert_kernel,
            [jax.ShapeDtypeStruct((slots, block + LANES), BF)] * 4
            + [jax.ShapeDtypeStruct((slots, units), BF)] * 3,
            (pos, msgs[k], wg, wu, wd),
            f"expert{k}",
        )
        dpgs.append(outs[4])
        dpus.append(outs[5])
        ghs.append(outs[6])
        arrived = [shift(outs[j], "y", j) for j in (1, 3, 2)]
        spread = call(
            expand_kernel,
            [jax.ShapeDtypeStruct((rows, block + LANES), BF)] * zs,
            (pos, msgs[k], outs[0], *arrived),
            f"expand{k}",
        )
        for j in range(zs):
            if offset == 0 and j == 0:
                pieces.append(spread[0])
            else:
                pieces.append(shift_two(spread[j], ("expert", "z"), (-offset, j)))
    mine = call(
        sum_kernel, jax.ShapeDtypeStruct((rows, block + LANES), BF), (pos, *pieces), "total"
    )
    slab, gate_grad = pl.pallas_call(
        rows_kernel,
        out_shape=[
            jax.ShapeDtypeStruct((tok_count, block), BF),
            jax.ShapeDtypeStruct((tok_count, 2), BF),
        ],
        in_specs=[smem()] + vmem(1 + zs),
        out_specs=vmem(2),
        scratch_shapes=[pltpu.VMEM((tok_count, LANES), F32)],
        name="rows",
    )(pos, expert_ids, mine, *[shift(mine, "z", j) for j in range(1, zs)])
    input_grad = call(
        columns_kernel,
        jax.ShapeDtypeStruct((tok_count, width), BF),
        (pos, slab, *[shift(slab, "y", offset) for offset in OFFSETS[1:]]),
        "columns",
    )
    away = half_gradients(pos, msgs, dpgs, dpus, ghs, True, None)
    received = [shift(part, "dp", 1) for part in away]
    grads = half_gradients(pos, msgs, dpgs, dpus, ghs, False, received)
    return (input_grad, gate_grad, grads[0][None], grads[1][None], grads[2][None])


def solution(mesh):
    dp, experts, tensor = (mesh.shape[name] for name in ("dp", "expert", "tensor"))
    view = Mesh(mesh.devices.reshape(dp, experts, tensor // 4, 4), ("dp", "expert", "z", "y"))
    row = P(("dp", "expert"), None)
    weight = P("expert", "dp", ("z", "y"))
    return jax.shard_map(
        on_device,
        mesh=view,
        in_specs=(row, row, row, row, weight, weight, weight),
        out_specs=(row, row, weight, weight, weight),
        check_vma=False,
    )
```

```python
import functools

import jax
import jax.numpy as jnp
from jax import lax
from jax.experimental import pallas as pl
from jax.experimental.pallas import tpu as pltpu
from jax.sharding import Mesh, PartitionSpec as P


BF = jnp.bfloat16
F32 = jnp.float32
NT = (((1,), (1,)), ((), ()))
TN = (((0,), (0,)), ((), ()))
LANES = 128


def vmem(count):
    return [pl.BlockSpec(memory_space=pltpu.VMEM)] * count


def smem():
    return pl.BlockSpec(memory_space=pltpu.SMEM)


def call(kernel, outs, operands, name):
    return pl.pallas_call(
        kernel,
        out_shape=outs,
        in_specs=[smem()] + vmem(len(operands) - 1),
        out_specs=jax.tree.map(lambda _: pl.BlockSpec(memory_space=pltpu.VMEM), outs),
        name=name,
    )(*operands)


def routing(pos, ids_ref, gw_ref, offsets):
    tokens = ids_ref.shape[1]
    ids = ids_ref[...]
    gates = gw_ref[...].astype(F32)
    before = (
        lax.broadcasted_iota(jnp.int32, (tokens, tokens), 0)
        < lax.broadcasted_iota(jnp.int32, (tokens, tokens), 1)
    ).astype(BF)
    rows = []
    weights = []
    for offset in offsets:
        hit = ids == lax.rem(pos[1] + offset + 4, 4)
        rows.append(jnp.max(hit.astype(F32), axis=0, keepdims=True))
        weights.append(jnp.sum(jnp.where(hit, gates, 0.0), axis=0, keepdims=True))
    member = jnp.concatenate(rows + [jnp.zeros((8 - len(rows), tokens), F32)], axis=0)
    rank = jnp.dot(member.astype(BF), before, preferred_element_type=F32)
    return member, rank, weights


def fill(out, pick, weight, tok, cot):
    tokens, width = tok.shape
    out[:, :width] = jnp.dot(pick, tok, preferred_element_type=F32).astype(BF)
    out[:, width : 2 * width] = jnp.dot(pick, cot, preferred_element_type=F32).astype(BF)
    token = lax.broadcasted_iota(jnp.int32, (8, tokens), 1).astype(F32) + 1.0
    line = lax.broadcasted_iota(jnp.int32, (8, tokens), 0)
    facts = jnp.where(line == 0, weight, jnp.where(line == 1, token, 0.0))
    facts = jnp.concatenate([facts, jnp.zeros((LANES - 8, tokens), F32)], axis=0).astype(BF)
    out[:, 2 * width :] = lax.dot_general(pick, facts, NT, preferred_element_type=F32).astype(BF)


def dispatch_kernel(offsets, quarter, pos, ids_ref, gw_ref, tok_ref, cot_ref, *outs):
    member, rank, weights = routing(pos, ids_ref, gw_ref, offsets)
    slots = outs[0].shape[0]
    slot = lax.broadcasted_iota(jnp.int32, (slots, tok_ref.shape[0]), 0)
    if quarter:
        slot = slot + pos[3] * slots
    slot = slot.astype(F32)
    for j, out in enumerate(outs):
        pick = jnp.where(
            (slot == rank[j : j + 1]) & (member[j : j + 1] > 0.5), 1.0, 0.0
        ).astype(BF)
        fill(out, pick, weights[j], tok_ref[...], cot_ref[...])


def expert_kernel(count, pos, *refs):
    msgs = refs[:count]
    wg_own, wg_sib, wu_own, wu_sib, wd_own, wd_sib = (ref.at[0] for ref in refs[count : count + 6])
    s_ref, dpg_ref, dpu_ref, gh_ref, facts_ref = refs[count + 6 :]
    half = wg_own.shape[0]
    width = 2 * half
    block = half // 2
    own = pl.multiple_of(pos[0] * half, LANES)
    sib = pl.multiple_of((1 - pos[0]) * half, LANES)

    def columns(at, size):
        parts = [msg[:, pl.ds(at, size)] for msg in msgs]
        return parts[0] if count == 1 else jnp.concatenate(parts, axis=0)

    x_own, x_sib = columns(own, half), columns(sib, half)
    facts = columns(2 * width, LANES)
    facts_ref[...] = facts
    g = facts[:, :1].astype(F32)

    def product(left_own, left_sib, w_own, w_sib):
        return jnp.dot(left_own, w_own[...], preferred_element_type=F32) + jnp.dot(
            left_sib, w_sib[...], preferred_element_type=F32
        )

    gate = product(x_own, x_sib, wg_own, wg_sib)
    up = product(x_own, x_sib, wu_own, wu_sib)
    back = product(columns(width + own, half), columns(width + sib, half), wd_own, wd_sib)
    sig = jax.nn.sigmoid(gate)
    act = gate * sig
    hid = act * up
    slot_gate = jnp.sum(hid.astype(BF).astype(F32) * back, axis=1, keepdims=True)
    hg = g * back
    dpg = (hg * up * sig * (1.0 + gate * (1.0 - sig))).astype(BF)
    dpu = (hg * act).astype(BF)
    dpg_ref[...] = dpg
    dpu_ref[...] = dpu
    gh_ref[...] = (g * hid).astype(BF)
    lane = lax.broadcasted_iota(jnp.int32, facts.shape, 1)
    extra = jnp.where(lane == pos[1], slot_gate, 0.0).astype(BF)
    for j in range(4):
        wg, wu = (wg_own, wu_own) if j < 2 else (wg_sib, wu_sib)
        at = (j % 2) * block
        part = lax.dot_general(dpg, wg[at : at + block, :], NT, preferred_element_type=F32)
        part += lax.dot_general(dpu, wu[at : at + block, :], NT, preferred_element_type=F32)
        s_ref[j, :, :block] = part.astype(BF)
        s_ref[j, :, block:] = extra


def expand_kernel(sizes, pos, *refs):
    n = len(sizes)
    out_ref = refs[-1]
    zs = out_ref.shape[0]
    rows = out_ref.shape[1] // sum(sizes)
    c = 0
    for k in range(n):
        got, facts = refs[k], refs[n + k]
        slots = got.shape[1] // sizes[k]
        for i in range(sizes[k]):
            at = slice(i * slots, (i + 1) * slots)
            total = got[0, at, :].astype(F32)
            for j in range(1, 4):
                total += got[j, at, :].astype(F32)
            index = facts[at, 1:2].astype(F32)
            token = lax.broadcasted_iota(jnp.int32, (slots, zs * rows), 1).astype(F32) + 1.0
            pick = jnp.where(index == token, 1.0, 0.0).astype(BF)
            spread = lax.dot_general(pick, total.astype(BF), TN, preferred_element_type=F32)
            spread = spread.astype(BF)
            for z in range(zs):
                out_ref[z, c * rows : (c + 1) * rows, :] = spread[z * rows : (z + 1) * rows]
            c += 1


def gather_kernel(pos, first_ref, second_ref, out_ref):
    rows = out_ref.shape[1]
    for ref, offsets in ((first_ref, (0, 2)), (second_ref, (1, -1))):
        total = ref[0].astype(F32)
        for z in range(1, ref.shape[0]):
            total += ref[z].astype(F32)
        for i, offset in enumerate(offsets):
            source = lax.rem(pos[1] - offset + 4, 4)
            out_ref[source] = total[i * rows : (i + 1) * rows].astype(BF)


def total_kernel(pos, got_ref, out_ref):
    total = got_ref[0].astype(F32)
    for j in range(1, got_ref.shape[0]):
        total += got_ref[j].astype(F32)
    total = total.astype(BF)
    for z in range(out_ref.shape[0]):
        out_ref[z] = total


def rows_kernel(pos, ids_ref, got_ref, slab_ref, gate_ref):
    width = slab_ref.shape[2]
    slab = got_ref[:, :width]
    for j in range(4):
        slab_ref[j] = slab
    values = got_ref[:, width:].astype(F32)
    lane = lax.broadcasted_iota(jnp.int32, values.shape, 1)
    ids = ids_ref[...]
    for k in range(2):
        mine = jnp.where(lane == ids[:, k : k + 1], values, 0.0)
        gate_ref[:, k : k + 1] = jnp.sum(mine, axis=1, keepdims=True).astype(BF)


def columns_kernel(pos, got_ref, out_ref):
    width = got_ref.shape[2]
    for j in range(4):
        at = pl.multiple_of(lax.rem(j + 2 * pos[0], 4) * width, LANES)
        out_ref[:, pl.ds(at, width)] = got_ref[j]


def grad_kernel(add, pos, *refs):
    xs, dys, gs, us, hs = refs[:4], refs[4:8], refs[8:11], refs[11:14], refs[14:17]
    rest = refs[17:]

    def stack(group):
        return jnp.concatenate([ref[...] for ref in group], axis=0)

    x = stack(xs)
    dy = stack(dys)
    for k, (left, right) in enumerate(((x, gs), (x, us), (dy, hs))):
        total = lax.dot_general(left, stack(right), TN, preferred_element_type=F32)
        if add:
            total += rest[k][...].astype(F32)
        rest[-3 + k][...] = total.astype(BF)


def half_gradients(pos, msgs, dpgs, dpus, ghs, other, received):
    slots = msgs[0].shape[0]
    units = dpgs[0].shape[1]
    width = (msgs[0].shape[1] - LANES) // 2
    half = width // 2
    step = 256
    count = half // step

    def first(pos):
        return (1 - pos[0]) if other else pos[0]

    x_spec = pl.BlockSpec((slots, step), lambda i, pos: (0, first(pos) * count + i))
    dy_spec = pl.BlockSpec((slots, step), lambda i, pos: (0, 2 * count + first(pos) * count + i))
    d_specs = [pl.BlockSpec(part.shape, lambda i, pos: (0, 0)) for part in dpgs]
    o_spec = pl.BlockSpec((step, units), lambda i, pos: (i, 0))
    return pl.pallas_call(
        functools.partial(grad_kernel, received is not None),
        out_shape=[jax.ShapeDtypeStruct((half, units), BF)] * 3,
        grid_spec=pltpu.PrefetchScalarGridSpec(
            num_scalar_prefetch=1,
            grid=(count,),
            in_specs=[x_spec] * 4 + [dy_spec] * 4 + d_specs * 3 + [o_spec] * len(received or ()),
            out_specs=[o_spec] * 3,
        ),
        name="grad_other" if other else "grad_own",
    )(pos, *msgs, *msgs, *dpgs, *dpus, *ghs, *(received or ()))


def shift(value, axis, offset):
    size = lax.axis_size(axis)
    return lax.ppermute(value, axis, [(i, (i + offset) % size) for i in range(size)])


def exchange(value, axis):
    return lax.all_to_all(value, axis, split_axis=0, concat_axis=0, tiled=True)


def after(value, *others):
    return lax.optimization_barrier((value, *others))[0]


def on_device(tokens, cotangent, gate_weights, expert_ids, w_gate, w_up, w_down):
    tok_count, width = tokens.shape
    slots = tok_count * 3 // 4
    units = w_gate.shape[2]
    block = width // 4
    zs = lax.axis_size("z")
    rows = tok_count // zs
    wide = block + LANES
    pos = jnp.stack(
        [lax.axis_index(name) for name in ("dp", "expert", "z", "y")]
    ).astype(jnp.int32)

    def array(*shape):
        return jax.ShapeDtypeStruct(shape, BF)

    ids_t, gates_t = expert_ids.T, gate_weights.T
    far = call(
        functools.partial(dispatch_kernel, (2,), True),
        [array(slots // 4, 2 * width + LANES)],
        (pos, ids_t, gates_t, tokens, cotangent),
        "dispatch_far",
    )[0]
    far = shift(far, "expert", 2)
    near = call(
        functools.partial(dispatch_kernel, (0, 1, -1), False),
        [array(slots, 2 * width + LANES)] * 3,
        (pos, ids_t, gates_t, tokens, cotangent),
        "dispatch_near",
    )
    weights = []
    for own in (w_gate, w_up, w_down):
        weights += [own, shift(own, "dp", 1)]
    plus, minus, far = lax.optimization_barrier((near[1], near[2], far))
    far = exchange(jnp.broadcast_to(far[None], (4, *far.shape)), "y")
    far = far.reshape(slots, 2 * width + LANES)
    plus, minus = shift(plus, "expert", 1), shift(minus, "expert", -1)

    def expert(msgs, name):
        n = slots * len(msgs)
        return call(
            functools.partial(expert_kernel, len(msgs)),
            [array(4, n, wide)] + [array(n, units)] * 3 + [array(n, LANES)],
            (pos, *msgs, *weights),
            name,
        )

    def expand(groups, sizes, name):
        return call(
            functools.partial(expand_kernel, sizes),
            array(zs, rows * sum(sizes), wide),
            (pos, *[got for got, _ in groups], *[facts for _, facts in groups]),
            name,
        )

    here = expert([near[0]], "expert_here")
    got_here = exchange(after(here[0], far), "y")
    there = expert([far], "expert_far")
    got_there = exchange(there[0], "y")
    sides = expert([plus, minus], "expert_sides")
    got_sides = exchange(sides[0], "y")
    first = exchange(
        expand([(got_here, here[4]), (got_there, there[4])], (1, 1), "expand_first"), "z"
    )
    second = expand([(got_sides, sides[4])], (2,), "expand_second")
    late = after(pos, second)
    second = exchange(second, "z")
    mine = exchange(call(gather_kernel, array(4, rows, wide), (pos, first, second), "gather"), "expert")
    mine = call(total_kernel, array(zs, rows, wide), (pos, mine), "total")
    mine = exchange(mine, "z").reshape(tok_count, wide)
    slab, gate_grad = call(
        rows_kernel, [array(4, tok_count, block), array(tok_count, 2)], (pos, expert_ids, mine), "rows"
    )
    input_grad = call(
        columns_kernel, array(tok_count, width), (pos, exchange(slab, "y")), "columns"
    )
    msgs = (near[0], far, plus, minus)
    dpgs, dpus, ghs = ([group[k] for group in (here, there, sides)] for k in (1, 2, 3))
    away = half_gradients(late, msgs, dpgs, dpus, ghs, True, None)
    received = [shift(part, "dp", 1) for part in away]
    grads = half_gradients(late, msgs, dpgs, dpus, ghs, False, received)
    return (input_grad, gate_grad, grads[0][None], grads[1][None], grads[2][None])


def solution(mesh):
    dp, experts, tensor = (mesh.shape[name] for name in ("dp", "expert", "tensor"))
    view = Mesh(mesh.devices.reshape(dp, experts, tensor // 4, 4), ("dp", "expert", "z", "y"))
    row = P(("dp", "expert"), None)
    weight = P("expert", "dp", ("z", "y"))
    return jax.shard_map(
        on_device,
        mesh=view,
        in_specs=(row, row, row, row, weight, weight, weight),
        out_specs=(row, row, weight, weight, weight),
        check_vma=False,
    )
```

```python
import functools

import jax
import jax.numpy as jnp
from jax import lax
from jax.experimental import pallas as pl
from jax.experimental.pallas import tpu as pltpu
from jax.sharding import Mesh, PartitionSpec as P


BF = jnp.bfloat16
F32 = jnp.float32
NT = (((1,), (1,)), ((), ()))
TN = (((0,), (0,)), ((), ()))
LANES = 128


MIB = 1 << 20


def array(*shape):
    return pltpu.VMEM(shape, BF)


def call(kernel, outs, operands, name, limit=16, scratch=()):
    here = pl.BlockSpec(memory_space=pltpu.VMEM)
    kept = [pltpu.with_memory_space_constraint(value, pltpu.VMEM) for value in operands[1:]]
    return pl.pallas_call(
        kernel,
        out_shape=outs,
        in_specs=[pl.BlockSpec(memory_space=pltpu.SMEM)] + [here] * len(kept),
        out_specs=[here] * len(outs),
        scratch_shapes=list(scratch),
        compiler_params=pltpu.CompilerParams(vmem_limit_bytes=limit * MIB),
        name=name,
    )(operands[0], *kept)


def routing(pos, ids_ref, gw_ref, offsets):
    tokens = ids_ref.shape[1]
    ids = ids_ref[...]
    gates = gw_ref[...].astype(F32)
    before = (
        lax.broadcasted_iota(jnp.int32, (tokens, tokens), 0)
        < lax.broadcasted_iota(jnp.int32, (tokens, tokens), 1)
    ).astype(BF)
    rows = []
    weights = []
    for offset in offsets:
        hit = ids == lax.rem(pos[1] + offset + 4, 4)
        rows.append(jnp.max(hit.astype(F32), axis=0, keepdims=True))
        weights.append(jnp.sum(jnp.where(hit, gates, 0.0), axis=0, keepdims=True))
    member = jnp.concatenate(rows + [jnp.zeros((8 - len(rows), tokens), F32)], axis=0)
    rank = jnp.dot(member.astype(BF), before, preferred_element_type=F32)
    return member, rank, weights


def picks(rank, member, j, slots, first):
    slot = lax.broadcasted_iota(jnp.int32, (slots, rank.shape[1]), 0)
    slot = (slot + first).astype(F32)
    hit = (slot == rank[j : j + 1]) & (member[j : j + 1] > 0.5)
    return jnp.where(hit, 1.0, 0.0).astype(BF)


def facts_of(pick, weight):
    tokens = pick.shape[1]
    token = lax.broadcasted_iota(jnp.int32, (8, tokens), 1).astype(F32) + 1.0
    line = lax.broadcasted_iota(jnp.int32, (8, tokens), 0)
    facts = jnp.where(line == 0, weight, jnp.where(line == 1, token, 0.0))
    facts = jnp.concatenate([facts, jnp.zeros((LANES - 8, tokens), F32)], axis=0).astype(BF)
    return lax.dot_general(pick, facts, NT, preferred_element_type=F32).astype(BF)


def far_kernel(pos, ids_ref, gw_ref, tok_ref, cot_ref, out):
    member, rank, weights = routing(pos, ids_ref, gw_ref, (2,))
    width = tok_ref.shape[1]
    slots = out.shape[0]
    pick = picks(rank, member, 0, slots, lax.rem(pos[3], 2) * slots)
    out[:, width:] = facts_of(pick, weights[0])

    @pl.when(pos[3] < 2)
    def _():
        out[:, :width] = jnp.dot(pick, tok_ref[...], preferred_element_type=F32).astype(BF)

    @pl.when(pos[3] >= 2)
    def _():
        out[:, :width] = jnp.dot(pick, cot_ref[...], preferred_element_type=F32).astype(BF)


def near_kernel(offsets, pos, ids_ref, gw_ref, tok_ref, cot_ref, *outs):
    member, rank, weights = routing(pos, ids_ref, gw_ref, offsets)
    width = tok_ref.shape[1]
    for j, out in enumerate(outs):
        pick = picks(rank, member, j, out.shape[0], 0)
        out[:, :width] = jnp.dot(pick, tok_ref[...], preferred_element_type=F32).astype(BF)
        out[:, width : 2 * width] = jnp.dot(
            pick, cot_ref[...], preferred_element_type=F32
        ).astype(BF)
        out[:, 2 * width :] = facts_of(pick, weights[j])


def expert_kernel(parts, pos, *refs):
    if parts:
        pieces, refs = refs[:4], refs[4:]
    else:
        msg, refs = refs[0], refs[1:]
    wg_own, wg_sib, wu_own, wu_sib, wd_own, wd_sib = (ref.at[0] for ref in refs[:6])
    refs = refs[6:]
    sends, (dpg_ref, dpu_ref, gh_ref, facts_ref) = refs[:4], refs[4:8]
    whole = refs[-1]
    half = wg_own.shape[0]
    width = 2 * half
    block = half // 2
    if parts:
        msg = refs[8]
        rows = pieces[0].shape[0]
        for piece, shift in zip(pieces, (0, 1, -1, 2)):
            source = lax.rem(pos[3] - shift + 4, 4)
            at = pl.multiple_of(lax.rem(source, 2) * rows, 16)
            column = pl.multiple_of(lax.div(source, 2) * width, LANES)
            msg[pl.ds(at, rows), pl.ds(column, width)] = piece[:, :width]
            msg[pl.ds(at, rows), 2 * width :] = piece[:, width:]
    own = pl.multiple_of(pos[0] * half, LANES)
    sib = pl.multiple_of((1 - pos[0]) * half, LANES)
    facts = msg[:, 2 * width :]
    facts_ref[...] = facts
    g = facts[:, :1].astype(F32)

    def product(base, w_own, w_sib):
        left = jnp.dot(msg[:, pl.ds(base + own, half)], w_own[...], preferred_element_type=F32)
        right = jnp.dot(msg[:, pl.ds(base + sib, half)], w_sib[...], preferred_element_type=F32)
        return left + right

    gate = product(0, wg_own, wg_sib)
    up = product(0, wu_own, wu_sib)
    back = product(width, wd_own, wd_sib)
    sig = jax.nn.sigmoid(gate)
    act = gate * sig
    hid = act * up
    slot_gate = jnp.sum(hid.astype(BF).astype(F32) * back, axis=1, keepdims=True)
    hg = g * back
    dpg = (hg * up * sig * (1.0 + gate * (1.0 - sig))).astype(BF)
    dpu = (hg * act).astype(BF)
    dpg_ref[...] = dpg
    dpu_ref[...] = dpu
    gh_ref[...] = (g * hid).astype(BF)
    lane = lax.broadcasted_iota(jnp.int32, facts.shape, 1)
    extra = jnp.where(lane == pos[1], slot_gate, 0.0).astype(BF)
    for j in range(4):
        wg, wu = (wg_own, wu_own) if j < 2 else (wg_sib, wu_sib)
        at = (j % 2) * block
        part = lax.dot_general(dpg, wg[at : at + block, :], NT, preferred_element_type=F32)
        part += lax.dot_general(dpu, wu[at : at + block, :], NT, preferred_element_type=F32)
        whole[j] = part.astype(BF)
    for j, send in enumerate(sends):
        send[:, :block] = whole[lax.rem(pos[3] + j, 4)]
        send[:, block:] = extra


def expand_kernel(chunks, pos, *refs):
    out_ref = refs[-1]
    zs = out_ref.shape[0]
    rows = out_ref.shape[1] // chunks
    for c in range(chunks):
        got, facts = refs[4 * c : 4 * c + 4], refs[4 * chunks + c]
        total = got[0][...].astype(F32)
        for part in got[1:]:
            total += part[...].astype(F32)
        index = facts[:, 1:2].astype(F32)
        token = lax.broadcasted_iota(jnp.int32, (total.shape[0], zs * rows), 1).astype(F32) + 1.0
        pick = jnp.where(index == token, 1.0, 0.0).astype(BF)
        spread = lax.dot_general(pick, total.astype(BF), TN, preferred_element_type=F32)
        spread = spread.astype(BF)
        for z in range(zs):
            out_ref[z, c * rows : (c + 1) * rows, :] = spread[z * rows : (z + 1) * rows]


def gather_kernel(pos, ref, *outs):
    rows = outs[0].shape[0]
    for i, out in enumerate(outs):
        total = ref[0, i * rows : (i + 1) * rows, :].astype(F32)
        for z in range(1, ref.shape[0]):
            total += ref[z, i * rows : (i + 1) * rows, :].astype(F32)
        out[...] = total.astype(BF)


def total_kernel(pos, *refs):
    out_ref = refs[-1]
    total = refs[0][...].astype(F32)
    for ref in refs[1:-1]:
        total += ref[...].astype(F32)
    total = total.astype(BF)
    for z in range(out_ref.shape[0]):
        out_ref[z] = total


def rows_kernel(pos, ids_ref, got_ref, slab_ref, gate_ref):
    width = slab_ref.shape[1]
    slab_ref[...] = got_ref[:, :width]
    values = got_ref[:, width:].astype(F32)
    lane = lax.broadcasted_iota(jnp.int32, values.shape, 1)
    ids = ids_ref[...]
    for k in range(2):
        mine = jnp.where(lane == ids[:, k : k + 1], values, 0.0)
        gate_ref[:, k : k + 1] = jnp.sum(mine, axis=1, keepdims=True).astype(BF)


def columns_kernel(pos, *refs):
    pieces, out_ref = refs[:4], refs[4]
    width = pieces[0].shape[1]
    for piece, shift in zip(pieces, (0, 1, -1, 2)):
        block = lax.rem(pos[3] - shift + 4 + 2 * pos[0], 4)
        out_ref[:, pl.ds(pl.multiple_of(block * width, LANES), width)] = piece[...]


def grad_kernel(other, pos, *refs):
    msgs, gs, us, hs = refs[:4], refs[4:8], refs[8:12], refs[12:16]
    added, outs = refs[16:-3], refs[-3:]
    half, units = outs[0].shape
    width = 2 * half
    base = ((1 - pos[0]) if other else pos[0]) * half
    step = 256

    def stack(group):
        return jnp.concatenate([ref[...] for ref in group], axis=0)

    rights = [stack(group) for group in (gs, us, hs)]
    for i in range(half // step):
        rows = slice(i * step, (i + 1) * step)

        def left(start):
            at = pl.multiple_of(start + base + i * step, LANES)
            return jnp.concatenate([msg[:, pl.ds(at, step)] for msg in msgs], axis=0)

        x, dy = left(0), left(width)
        for k, value in enumerate((x, x, dy)):
            total = lax.dot_general(value, rights[k], TN, preferred_element_type=F32)
            if added:
                total += added[k][rows].astype(F32)
            outs[k][rows] = total.astype(BF)


def shift(value, axis, offset):
    size = lax.axis_size(axis)
    return lax.ppermute(value, axis, [(i, (i + offset) % size) for i in range(size)])


def exchange(value, axis):
    return lax.all_to_all(value, axis, split_axis=0, concat_axis=0, tiled=True)


def after(value, *others):
    return lax.optimization_barrier((value, *others))[0]


def on_device(tokens, cotangent, gate_weights, expert_ids, w_gate, w_up, w_down):
    tok_count, width = tokens.shape
    slots = tok_count * 3 // 4
    units = w_gate.shape[2]
    block = width // 4
    zs = lax.axis_size("z")
    rows = tok_count // zs
    wide = block + LANES
    long = 2 * width + LANES
    pos = jnp.stack(
        [lax.axis_index(name) for name in ("dp", "expert", "z", "y")]
    ).astype(jnp.int32)
    given = (pos, expert_ids.T, gate_weights.T, tokens, cotangent)

    (far,) = call(far_kernel, [array(slots // 2, width + LANES)], given, "dispatch_far")
    far = shift(far, "expert", 2)
    plus, minus = call(
        functools.partial(near_kernel, (1, -1)), [array(slots, long)] * 2, given, "dispatch_near"
    )
    plus, minus = shift(plus, "expert", 1), shift(minus, "expert", -1)
    (here,) = call(functools.partial(near_kernel, (0,)), [array(slots, long)], given, "dispatch_here")
    weights = []
    for own in (w_gate, w_up, w_down):
        weights += [own, shift(own, "dp", 1)]
    far = [far] + [shift(far, "y", offset) for offset in (1, -1, 2)]

    def expert(msgs, name):
        parts = len(msgs) > 1
        return call(
            functools.partial(expert_kernel, parts),
            [array(slots, wide)] * 4
            + [array(slots, units)] * 3
            + [array(slots, LANES)]
            + [array(slots, long)] * parts,
            (pos, *msgs, *weights),
            name,
            limit=24,
            scratch=[pltpu.VMEM((4, slots, block), BF)],
        )

    def scatter(sends):
        return [sends[0]] + [shift(sends[j], "y", j) for j in (1, 3, 2)]

    def expand(groups, facts, name):
        return call(
            functools.partial(expand_kernel, len(groups)),
            [array(zs, rows * len(groups), wide)],
            (pos, *[part for group in groups for part in group], *facts),
            name,
        )[0]

    local = expert([here], "expert_here")
    local_sends = lax.optimization_barrier((*local[:4], *far))
    far = local_sends[4:]
    local_got = scatter(local_sends[:4])
    remote = expert(far, "expert_far")
    remote_got = scatter(remote[:4])
    right = expert([plus], "expert_plus")
    right_got = scatter(right[:4])
    left = expert([minus], "expert_minus")
    left_got = scatter(left[:4])
    first = expand((local_got, remote_got), (local[7], remote[7]), "expand_first")
    early = after(pos, first, left[0])
    second = expand((right_got, left_got), (right[7], left[7]), "expand_second")
    late = after(pos, second)
    mine = list(call(gather_kernel, [array(rows, wide)] * 2, (pos, exchange(first, "z")), "gather_first"))
    mine += call(gather_kernel, [array(rows, wide)] * 2, (pos, exchange(second, "z")), "gather_second")
    mine = [mine[0]] + [shift(mine[k], "expert", -offset) for k, offset in ((1, 2), (2, 1), (3, -1))]
    (mine,) = call(total_kernel, [array(zs, rows, wide)], (pos, *mine), "total")
    mine = exchange(mine, "z").reshape(tok_count, wide)
    slab, gate_grad = call(
        rows_kernel,
        [array(tok_count, block), jax.ShapeDtypeStruct((tok_count, 2), BF)],
        (pos, expert_ids, mine),
        "rows",
    )
    (input_grad,) = call(
        columns_kernel,
        [jax.ShapeDtypeStruct((tok_count, width), BF)],
        (pos, slab, *[shift(slab, "y", offset) for offset in (1, -1, 2)]),
        "columns",
    )
    chunks = (local, remote, right, left)
    used = [here, remote[8], plus, minus] + [chunk[k] for k in (4, 5, 6) for chunk in chunks]
    half = width // 2
    away = call(
        functools.partial(grad_kernel, True), [array(half, units)] * 3, (early, *used), "grad_other", limit=24
    )
    received = [shift(part, "dp", 1) for part in away]
    grads = call(
        functools.partial(grad_kernel, False),
        [jax.ShapeDtypeStruct((half, units), BF)] * 3,
        (late, *used, *received),
        "grad_own",
        limit=24,
    )
    return (input_grad, gate_grad, grads[0][None], grads[1][None], grads[2][None])


def solution(mesh):
    dp, experts, tensor = (mesh.shape[name] for name in ("dp", "expert", "tensor"))
    view = Mesh(mesh.devices.reshape(dp, experts, tensor // 4, 4), ("dp", "expert", "z", "y"))
    row = P(("dp", "expert"), None)
    weight = P("expert", "dp", ("z", "y"))
    return jax.shard_map(
        on_device,
        mesh=view,
        in_specs=(row, row, row, row, weight, weight, weight),
        out_specs=(row, row, weight, weight, weight),
        check_vma=False,
    )
```

```python
import functools

import jax
import jax.numpy as jnp
from jax import lax
from jax.experimental import pallas as pl
from jax.experimental.pallas import tpu as pltpu
from jax.sharding import Mesh, PartitionSpec as P


BF = jnp.bfloat16
F32 = jnp.float32
NT = (((1,), (1,)), ((), ()))
TN = (((0,), (0,)), ((), ()))
LANES = 128


MIB = 1 << 20


def array(*shape):
    return pltpu.VMEM(shape, BF)


def plain(*shape):
    return pltpu.HBM(shape, BF)


def call(kernel, outs, operands, limit=8, scratch=(), free=(), unblocked=()):
    spec = pl.BlockSpec(memory_space=pltpu.VMEM)
    specs = [pl.BlockSpec(memory_space=pltpu.SMEM)]
    kept = [operands[0]]
    for k, value in enumerate(operands[1:]):
        if k in unblocked:
            specs.append(pl.BlockSpec(memory_space=pl.ANY))
        else:
            specs.append(spec)
            space = pltpu.HBM if k in free else pltpu.VMEM
            value = pltpu.with_memory_space_constraint(value, space)
        kept.append(value)
    return pl.pallas_call(
        kernel,
        out_shape=outs,
        in_specs=specs,
        out_specs=[spec] * len(outs),
        scratch_shapes=list(scratch),
        compiler_params=pltpu.CompilerParams(vmem_limit_bytes=limit * MIB),
    )(*kept)


def routing(pos, ids_ref, gw_ref, offsets):
    tokens = ids_ref.shape[1]
    ids = ids_ref[...]
    gates = gw_ref[...].astype(F32)
    before = (
        lax.broadcasted_iota(jnp.int32, (tokens, tokens), 0)
        < lax.broadcasted_iota(jnp.int32, (tokens, tokens), 1)
    ).astype(BF)
    rows = []
    weights = []
    for offset in offsets:
        hit = ids == lax.rem(pos[1] + offset + 4, 4)
        rows.append(jnp.max(hit.astype(F32), axis=0, keepdims=True))
        weights.append(jnp.sum(jnp.where(hit, gates, 0.0), axis=0, keepdims=True))
    member = jnp.concatenate(rows + [jnp.zeros((8 - len(rows), tokens), F32)], axis=0)
    rank = jnp.dot(member.astype(BF), before, preferred_element_type=F32)
    return member, rank, weights


def picks(rank, member, j, slots, first):
    slot = lax.broadcasted_iota(jnp.int32, (slots, rank.shape[1]), 0)
    slot = (slot + first).astype(F32)
    hit = (slot == rank[j : j + 1]) & (member[j : j + 1] > 0.5)
    return jnp.where(hit, 1.0, 0.0).astype(BF)


def facts_of(pick, weight):
    tokens = pick.shape[1]
    token = lax.broadcasted_iota(jnp.int32, (8, tokens), 1).astype(F32) + 1.0
    line = lax.broadcasted_iota(jnp.int32, (8, tokens), 0)
    facts = jnp.where(line == 0, weight, jnp.where(line == 1, token, 0.0))
    facts = jnp.concatenate([facts, jnp.zeros((LANES - 8, tokens), F32)], axis=0).astype(BF)
    return lax.dot_general(pick, facts, NT, preferred_element_type=F32).astype(BF)


def far_kernel(pos, ids_ref, gw_ref, tok_ref, cot_ref, out, held, sem):
    first = pos[3] < 2

    @pl.when(first)
    def _():
        pltpu.make_async_copy(tok_ref, held, sem).start()

    @pl.when(jnp.logical_not(first))
    def _():
        pltpu.make_async_copy(cot_ref, held, sem).start()

    member, rank, weights = routing(pos, ids_ref, gw_ref, (2,))
    width = tok_ref.shape[1]
    slots = out.shape[0]
    pick = picks(rank, member, 0, slots, lax.rem(pos[3], 2) * slots)
    out[:, width:] = facts_of(pick, weights[0])
    pltpu.make_async_copy(tok_ref, held, sem).wait()
    out[:, :width] = jnp.dot(pick, held[...], preferred_element_type=F32).astype(BF)


def near_kernel(offsets, pos, ids_ref, gw_ref, tok_ref, cot_ref, *outs):
    member, rank, weights = routing(pos, ids_ref, gw_ref, offsets)
    width = tok_ref.shape[1]
    for j, out in enumerate(outs):
        pick = picks(rank, member, j, out.shape[0], 0)
        out[:, :width] = jnp.dot(pick, tok_ref[...], preferred_element_type=F32).astype(BF)
        out[:, width : 2 * width] = jnp.dot(
            pick, cot_ref[...], preferred_element_type=F32
        ).astype(BF)
        out[:, 2 * width :] = facts_of(pick, weights[j])


def expert_kernel(kind, pos, *refs):
    count = {"here": 1, "far": 4, "sides": 2}[kind]
    pieces, refs = refs[:count], refs[count:]
    wg_own, wg_sib, wu_own, wu_sib, wd_own, wd_sib = (ref.at[0] for ref in refs[:6])
    sends, aux_ref, whole = refs[6:10], refs[10], refs[-1]
    half, units = wg_own.shape
    width = 2 * half
    block = half // 2
    if kind == "far":
        msgs = [refs[11]]
        rows = pieces[0].shape[0]
        for piece, shift in zip(pieces, (0, 1, -1, 2)):
            source = lax.rem(pos[3] - shift + 4, 4)
            at = pl.multiple_of(lax.rem(source, 2) * rows, 16)
            column = pl.multiple_of(lax.div(source, 2) * width, LANES)
            msgs[0][pl.ds(at, rows), pl.ds(column, width)] = piece[:, :width]
            msgs[0][pl.ds(at, rows), 2 * width :] = piece[:, width:]
    else:
        msgs = pieces
    own = pl.multiple_of(pos[0] * half, LANES)
    sib = pl.multiple_of((1 - pos[0]) * half, LANES)

    def columns(at, size):
        parts = [msg[:, pl.ds(at, size)] for msg in msgs]
        return parts[0] if len(parts) == 1 else jnp.concatenate(parts, axis=0)

    facts = columns(2 * width, LANES)
    g = facts[:, :1].astype(F32)

    def product(left_own, left_sib, w_own, w_sib):
        left = jnp.dot(left_own, w_own[...], preferred_element_type=F32)
        return left + jnp.dot(left_sib, w_sib[...], preferred_element_type=F32)

    x_own, x_sib = columns(own, half), columns(sib, half)
    gate = product(x_own, x_sib, wg_own, wg_sib)
    up = product(x_own, x_sib, wu_own, wu_sib)
    back = product(columns(width + own, half), columns(width + sib, half), wd_own, wd_sib)
    sig = jax.nn.sigmoid(gate)
    act = gate * sig
    hid = act * up
    slot_gate = jnp.sum(hid.astype(BF).astype(F32) * back, axis=1, keepdims=True)
    hg = g * back
    dpg = (hg * up * sig * (1.0 + gate * (1.0 - sig))).astype(BF)
    dpu = (hg * act).astype(BF)
    aux_ref[:, :units] = dpg
    aux_ref[:, units : 2 * units] = dpu
    aux_ref[:, 2 * units : 3 * units] = (g * hid).astype(BF)
    aux_ref[:, 3 * units :] = facts
    lane = lax.broadcasted_iota(jnp.int32, facts.shape, 1)
    extra = jnp.where(lane == pos[1], slot_gate, 0.0).astype(BF)
    for j in range(4):
        wg, wu = (wg_own, wu_own) if j < 2 else (wg_sib, wu_sib)
        at = (j % 2) * block
        part = lax.dot_general(dpg, wg[at : at + block, :], NT, preferred_element_type=F32)
        part += lax.dot_general(dpu, wu[at : at + block, :], NT, preferred_element_type=F32)
        whole[j] = part.astype(BF)
    for j, send in enumerate(sends):
        send[:, :block] = whole[lax.rem(pos[3] + j, 4)]
        send[:, block:] = extra


def expand_kernel(pos, a_ref, b_ref, c_ref, d_ref, aux_ref, *outs):
    tokens = outs[0].shape[0]
    slots = a_ref.shape[0] // len(outs)
    token = lax.broadcasted_iota(jnp.int32, (slots, tokens), 1).astype(F32) + 1.0
    for i, out in enumerate(outs):
        at = slice(i * slots, (i + 1) * slots)
        total = a_ref[at, :].astype(F32)
        for ref in (b_ref, c_ref, d_ref):
            total += ref[at, :].astype(F32)
        index = aux_ref[at, aux_ref.shape[1] - LANES :][:, 1:2].astype(F32)
        pick = jnp.where(index == token, 1.0, 0.0).astype(BF)
        out[...] = lax.dot_general(
            pick, total.astype(BF), TN, preferred_element_type=F32
        ).astype(BF)


def total_kernel(pos, *refs):
    out_ref = refs[-1]
    rows = out_ref.shape[1]
    for z in range(out_ref.shape[0]):
        at = slice(z * rows, (z + 1) * rows)
        total = refs[0][at, :].astype(F32)
        for ref in refs[1:-1]:
            total += ref[at, :].astype(F32)
        out_ref[z] = total.astype(BF)


def gather_kernel(pos, got_ref, out_ref):
    total = got_ref[0].astype(F32)
    for z in range(1, got_ref.shape[0]):
        total += got_ref[z].astype(F32)
    total = total.astype(BF)
    for z in range(out_ref.shape[0]):
        out_ref[z] = total


def rows_kernel(pos, ids_ref, got_ref, slab_ref, gate_ref):
    width = slab_ref.shape[1]
    slab_ref[...] = got_ref[:, :width]
    eye = lax.broadcasted_iota(jnp.int32, (8, LANES), 0) == lax.broadcasted_iota(
        jnp.int32, (8, LANES), 1
    )
    values = lax.dot_general(
        jnp.where(eye, 1.0, 0.0).astype(BF), got_ref[:, width:], NT, preferred_element_type=F32
    )
    ids = ids_ref[...]
    line = lax.broadcasted_iota(jnp.int32, values.shape, 0)
    for k in range(2):
        mine = jnp.where(line == ids[k : k + 1], values, 0.0)
        gate_ref[k : k + 1] = jnp.sum(mine, axis=0, keepdims=True).astype(BF)


def columns_kernel(pos, *refs):
    pieces, out_ref = refs[:4], refs[4]
    width = pieces[0].shape[1]
    for piece, shift in zip(pieces, (0, 1, -1, 2)):
        block = lax.rem(pos[3] - shift + 4 + 2 * pos[0], 4)
        out_ref[:, pl.ds(pl.multiple_of(block * width, LANES), width)] = piece[...]


def grad_kernel(other, pos, here_ref, far_ref, plus_ref, minus_ref, *refs):
    msgs = (here_ref, far_ref, plus_ref, minus_ref)
    auxs, added, outs = refs[:3], refs[3:-3], refs[-3:]
    half, units = outs[0].shape
    width = 2 * half
    base = ((1 - pos[0]) if other else pos[0]) * half
    step = 256
    right = jnp.concatenate([ref[:, : 2 * units] for ref in auxs], axis=0)
    hidden = jnp.concatenate([ref[:, 2 * units : 3 * units] for ref in auxs], axis=0)
    for i in range(half // step):
        rows = slice(i * step, (i + 1) * step)

        def left(start):
            at = pl.multiple_of(start + base + i * step, LANES)
            return jnp.concatenate([msg[:, pl.ds(at, step)] for msg in msgs], axis=0)

        both = lax.dot_general(left(0), right, TN, preferred_element_type=F32)
        down = lax.dot_general(left(width), hidden, TN, preferred_element_type=F32)
        for k, total in enumerate((both[:, :units], both[:, units:], down)):
            if added:
                total += added[k][rows].astype(F32)
            outs[k][rows] = total.astype(BF)


def shift(value, axis, offset):
    size = lax.axis_size(axis)
    return lax.ppermute(value, axis, [(i, (i + offset) % size) for i in range(size)])


def exchange(value, axis):
    return lax.all_to_all(value, axis, split_axis=0, concat_axis=0, tiled=True)


def after(value, *others):
    return lax.optimization_barrier((value, *others))[0]


def on_device(tokens, cotangent, gate_weights, expert_ids, w_gate, w_up, w_down):
    tok_count, width = tokens.shape
    slots = tok_count * 3 // 4
    units = w_gate.shape[2]
    block = width // 4
    zs = lax.axis_size("z")
    rows = tok_count // zs
    wide = block + LANES
    long = 2 * width + LANES
    pos = jnp.stack(
        [lax.axis_index(name) for name in ("dp", "expert", "z", "y")]
    ).astype(jnp.int32)
    given = (expert_ids.T, gate_weights.T, tokens, cotangent)

    (far,) = call(
        far_kernel,
        [array(slots // 2, width + LANES)],
        (pos, *given),
        free=(0, 1),
        unblocked=(2, 3),
        scratch=[pltpu.VMEM(tokens.shape, BF), pltpu.SemaphoreType.DMA],
    )
    plus, minus = call(
        functools.partial(near_kernel, (1, -1)),
        [array(slots, long)] * 2,
        (after(pos, far), *given),
        free=(0, 1),
    )
    then = after(pos, plus)
    (here,) = call(
        functools.partial(near_kernel, (0,)), [array(slots, long)], (then, *given),
        free=(0, 1),
    )
    weights = []
    for own in (w_gate, w_up, w_down):
        weights += [own, shift(after(own, plus), "dp", 1)]
    plus, minus = shift(plus, "expert", 1), shift(minus, "expert", -1)
    far = shift(far, "expert", 2)
    far = [far] + [shift(far, "y", offset) for offset in (1, -1, 2)]

    def expert(pos, msgs, kind):
        n = slots * (2 if kind == "sides" else 1)
        return call(
            functools.partial(expert_kernel, kind),
            [array(n, wide)] * 4
            + [plain(n, 3 * units + LANES)]
            + [array(slots, long)] * (kind == "far"),
            (pos, *msgs, *weights),
            scratch=[pltpu.VMEM((4, n, block), BF)],
        )

    def scatter(sends):
        return [sends[0]] + [shift(sends[j], "y", j) for j in (1, 3, 2)]

    def expand(pos, got, aux):
        count = aux.shape[0] // slots
        return call(expand_kernel, [array(tok_count, wide)] * count, (pos, *got, aux))

    local = expert(pos, [here], "here")
    remote = expert(after(pos, local[0]), far, "far")
    then = after(pos, remote[0])
    sides = expert(then, [plus, minus], "sides")
    (mine,) = expand(then, scatter(local[:4]), local[4])
    then = after(pos, sides[0])
    (from_far,) = expand(then, scatter(remote[:4]), remote[4])
    from_plus, from_minus = expand(then, scatter(sides[:4]), sides[4])
    early = after(pos, from_far)
    parts = [
        mine,
        shift(from_far, "expert", 2),
        shift(from_plus, "expert", -1),
        shift(from_minus, "expert", 1),
    ]
    (mine,) = call(total_kernel, [plain(zs, rows, wide)], (pos, *parts))
    late = after(pos, mine)
    (mine,) = call(gather_kernel, [plain(zs, rows, wide)], (pos, exchange(mine, "z")))
    mine = exchange(mine, "z").reshape(tok_count, wide)
    slab, gate_grad = call(
        rows_kernel, [array(tok_count, block), plain(2, tok_count)], (pos, expert_ids.T, mine)
    )
    (input_grad,) = call(
        columns_kernel,
        [plain(tok_count, width)],
        (pos, slab, *[shift(slab, "y", offset) for offset in (1, -1, 2)]),
    )
    used = [here, remote[5], plus, minus, local[4], remote[4], sides[4]]
    half = width // 2
    away = call(
        functools.partial(grad_kernel, True), [array(half, units)] * 3, (early, *used),
        limit=12,
    )
    received = [shift(part, "dp", 1) for part in away]
    grads = call(
        functools.partial(grad_kernel, False), [plain(half, units)] * 3, (late, *used, *received),
        limit=12,
    )
    return (input_grad, gate_grad.T, grads[0][None], grads[1][None], grads[2][None])


def solution(mesh):
    dp, experts, tensor = (mesh.shape[name] for name in ("dp", "expert", "tensor"))
    view = Mesh(mesh.devices.reshape(dp, experts, tensor // 4, 4), ("dp", "expert", "z", "y"))
    row = P(("dp", "expert"), None)
    weight = P("expert", "dp", ("z", "y"))

    return jax.shard_map(
        on_device,
        mesh=view,
        in_specs=(row, row, row, row, weight, weight, weight),
        out_specs=(row, row, weight, weight, weight),
        check_vma=False,
    )
```

```python
import functools

import jax
import jax.numpy as jnp
from jax import lax
from jax.experimental import pallas as pl
from jax.experimental.pallas import tpu as pltpu
from jax.sharding import Mesh, PartitionSpec as P


BF = jnp.bfloat16
F32 = jnp.float32
NT = (((1,), (1,)), ((), ()))
TN = (((0,), (0,)), ((), ()))
LANES = 128
OFFSETS = (0, 1, -1, 2)


MIB = 1 << 20


def array(*shape):
    return pltpu.VMEM(shape, BF)


def plain(*shape):
    return pltpu.HBM(shape, BF)


def call(kernel, outs, operands, limit=8, scratch=(), free=(), unblocked=()):
    spec = pl.BlockSpec(memory_space=pltpu.VMEM)
    specs = [pl.BlockSpec(memory_space=pltpu.SMEM)]
    kept = [operands[0]]
    for k, value in enumerate(operands[1:]):
        specs.append(pl.BlockSpec(memory_space=pl.ANY) if k in unblocked else spec)
        space = pltpu.HBM if k in free else pltpu.VMEM
        kept.append(pltpu.with_memory_space_constraint(value, space))
    return pl.pallas_call(
        kernel,
        out_shape=outs,
        in_specs=specs,
        out_specs=[spec] * len(outs),
        scratch_shapes=list(scratch),
        compiler_params=pltpu.CompilerParams(vmem_limit_bytes=limit * MIB),
    )(*kept)


def routing(pos, ids_ref, offsets):
    tokens = ids_ref.shape[1]
    ids = ids_ref[...]
    before = (
        lax.broadcasted_iota(jnp.int32, (tokens, tokens), 0)
        < lax.broadcasted_iota(jnp.int32, (tokens, tokens), 1)
    ).astype(BF)
    hits = [ids == lax.rem(pos[1] + offset + 4, 4) for offset in offsets]
    rows = [jnp.max(hit.astype(F32), axis=0, keepdims=True) for hit in hits]
    member = jnp.concatenate(rows + [jnp.zeros((8 - len(rows), tokens), F32)], axis=0)
    rank = jnp.dot(member.astype(BF), before, preferred_element_type=F32)
    return member, rank, hits


def picks(rank, member, j, slots, first):
    slot = lax.broadcasted_iota(jnp.int32, (slots, rank.shape[1]), 0)
    slot = (slot + first).astype(F32)
    hit = (slot == rank[j : j + 1]) & (member[j : j + 1] > 0.5)
    return jnp.where(hit, 1.0, 0.0).astype(BF)


def facts_of(pick, hit, gw_ref):
    tokens = pick.shape[1]
    weight = jnp.sum(jnp.where(hit, gw_ref[...].astype(F32), 0.0), axis=0, keepdims=True)
    facts = jnp.where(lax.broadcasted_iota(jnp.int32, (LANES, tokens), 0) == 0, weight, 0.0)
    return lax.dot_general(pick, facts.astype(BF), NT, preferred_element_type=F32).astype(BF)


def far_kernel(pos, ids_ref, gw_ref, tok_ref, cot_ref, out, tok_out, cot_out, sems):
    copies = [
        pltpu.make_async_copy(tok_ref, tok_out, sems.at[0]),
        pltpu.make_async_copy(cot_ref, cot_out, sems.at[1]),
    ]
    for copy in copies:
        copy.start()
    member, rank, hits = routing(pos, ids_ref, (2,))
    width = tok_ref.shape[1]
    slots = out.shape[0]
    pick = picks(rank, member, 0, slots, lax.rem(pos[3], 2) * slots)
    out[:, width:] = facts_of(pick, hits[0], gw_ref)
    for copy in copies:
        copy.wait()

    @pl.when(pos[3] < 2)
    def _():
        out[:, :width] = jnp.dot(pick, tok_out[...], preferred_element_type=F32).astype(BF)

    @pl.when(pos[3] >= 2)
    def _():
        out[:, :width] = jnp.dot(pick, cot_out[...], preferred_element_type=F32).astype(BF)


def near_kernel(offsets, pos, ids_ref, gw_ref, tok_ref, cot_ref, *outs):
    member, rank, hits = routing(pos, ids_ref, offsets)
    width = tok_ref.shape[1]
    for j, out in enumerate(outs):
        pick = picks(rank, member, j, out.shape[0], 0)
        out[:, :width] = jnp.dot(pick, tok_ref[...], preferred_element_type=F32).astype(BF)
        out[:, width : 2 * width] = jnp.dot(
            pick, cot_ref[...], preferred_element_type=F32
        ).astype(BF)
        out[:, 2 * width :] = facts_of(pick, hits[j], gw_ref)


def expert_kernel(kind, pos, *refs):
    count = {"here": 1, "far": 4, "sides": 2}[kind]
    pieces, refs = refs[:count], refs[count:]
    wg_own, wg_sib, wu_own, wu_sib, wd_own, wd_sib = (ref.at[0] for ref in refs[:6])
    ends = 14 if kind == "sides" else 10
    sends, aux_ref, whole = refs[6:ends], refs[ends], refs[-1]
    half, units = wg_own.shape
    width = 2 * half
    block = half // 2
    if kind == "far":
        msgs = [refs[ends + 1]]
        rows = pieces[0].shape[0]
        for piece, shift in zip(pieces, (0, 1, -1, 2)):
            source = lax.rem(pos[3] - shift + 4, 4)
            at = pl.multiple_of(lax.rem(source, 2) * rows, 16)
            column = pl.multiple_of(lax.div(source, 2) * width, LANES)
            msgs[0][pl.ds(at, rows), pl.ds(column, width)] = piece[:, :width]
            msgs[0][pl.ds(at, rows), 2 * width :] = piece[:, width:]
    else:
        msgs = pieces
    own = pl.multiple_of(pos[0] * half, LANES)
    sib = pl.multiple_of((1 - pos[0]) * half, LANES)

    def columns(at, size):
        parts = [msg[:, pl.ds(at, size)] for msg in msgs]
        return parts[0] if len(parts) == 1 else jnp.concatenate(parts, axis=0)

    facts = columns(2 * width, LANES)
    g = facts[:, :1].astype(F32)

    def product(left_own, left_sib, w_own, w_sib):
        left = jnp.dot(left_own, w_own[...], preferred_element_type=F32)
        return left + jnp.dot(left_sib, w_sib[...], preferred_element_type=F32)

    x_own, x_sib = columns(own, half), columns(sib, half)
    gate = product(x_own, x_sib, wg_own, wg_sib)
    up = product(x_own, x_sib, wu_own, wu_sib)
    back = product(columns(width + own, half), columns(width + sib, half), wd_own, wd_sib)
    sig = jax.nn.sigmoid(gate)
    act = gate * sig
    hid = act * up
    share = hid.astype(BF).astype(F32) * back
    hg = g * back
    dpg = (hg * up * sig * (1.0 + gate * (1.0 - sig))).astype(BF)
    dpu = (hg * act).astype(BF)
    aux_ref[:, :units] = dpg
    aux_ref[:, units : 2 * units] = dpu
    aux_ref[:, 2 * units : 3 * units] = (g * hid).astype(BF)
    for j in range(4):
        wg, wu = (wg_own, wu_own) if j < 2 else (wg_sib, wu_sib)
        at = (j % 2) * block
        part = lax.dot_general(dpg, wg[at : at + block, :], NT, preferred_element_type=F32)
        part += lax.dot_general(dpu, wu[at : at + block, :], NT, preferred_element_type=F32)
        whole[j] = part.astype(BF)
    slots = sends[0].shape[0] - 8
    for c in range(len(sends) // 4):
        at = slice(c * slots, (c + 1) * slots)
        padded = jnp.concatenate([share[at], jnp.zeros((LANES - slots, units), F32)], axis=0)
        line = lax.dot_general(
            jnp.ones((8, units), F32), padded, NT,
            precision=lax.Precision.HIGHEST, preferred_element_type=F32,
        ).astype(BF)
        for j in range(4):
            send = sends[4 * c + j]
            send[:slots] = whole[lax.rem(pos[3] + j, 4), at, :]
            send[slots:, :LANES] = line
            send[slots:, LANES:] = jnp.zeros((8, block - LANES), BF)


def combine_kernel(pos, ids_ref, *refs):
    out_ref = refs[-1]
    zs, rows, wide = out_ref.shape
    tokens = zs * rows
    width = wide - LANES
    slots = refs[0].shape[0] - 8
    member, rank, _ = routing(pos, ids_ref, OFFSETS)
    result = jnp.zeros((tokens, width), F32)
    gates = []
    for k in range(4):
        group = refs[4 * k : 4 * k + 4]
        total = group[0][...].astype(F32)
        for ref in group[1:]:
            total += ref[...].astype(F32)
        total = total.astype(BF)
        pick = picks(rank, member, k, slots, 0)
        result += lax.dot_general(pick, total[:slots], TN, preferred_element_type=F32)
        pick = picks(rank, member, k, LANES, 0)
        line = jnp.dot(total[slots:, :LANES], pick, preferred_element_type=F32)
        gates.append(line[:1])
    gates = jnp.concatenate(gates + [jnp.zeros((rows - 4, tokens), F32)], axis=0).astype(BF)
    result = result.astype(BF)
    for z in range(zs):
        out_ref[z, :, :width] = result[z * rows : (z + 1) * rows]
        out_ref[z, :, width:] = gates


def gather_kernel(pos, ids_ref, got_ref, out_ref, gate_ref):
    width = out_ref.shape[2]
    total = got_ref[0].astype(F32)
    for z in range(1, got_ref.shape[0]):
        total += got_ref[z].astype(F32)
    slab = total[:, :width].astype(BF)
    for z in range(out_ref.shape[0]):
        out_ref[z] = slab
    ids = ids_ref[...]
    gates = jnp.zeros(ids.shape, F32)
    for k, offset in enumerate(OFFSETS):
        hit = ids == lax.rem(pos[1] + offset + 4, 4)
        gates += jnp.where(hit, total[k : k + 1, width:], 0.0)
    gate_ref[...] = gates.astype(BF)


def columns_kernel(pos, *refs):
    pieces, out_ref = refs[:4], refs[4]
    width = pieces[0].shape[1]
    for piece, shift in zip(pieces, (0, 1, -1, 2)):
        block = lax.rem(pos[3] - shift + 4 + 2 * pos[0], 4)
        out_ref[:, pl.ds(pl.multiple_of(block * width, LANES), width)] = piece[...]


def grad_kernel(other, pos, here_ref, far_ref, plus_ref, minus_ref, *refs):
    msgs = (here_ref, far_ref, plus_ref, minus_ref)
    auxs, added, outs = refs[:3], refs[3:-3], refs[-3:]
    half, units = outs[0].shape
    width = 2 * half
    base = ((1 - pos[0]) if other else pos[0]) * half
    step = 256
    right = jnp.concatenate([ref[:, : 2 * units] for ref in auxs], axis=0)
    hidden = jnp.concatenate([ref[:, 2 * units : 3 * units] for ref in auxs], axis=0)
    for i in range(half // step):
        rows = slice(i * step, (i + 1) * step)

        def left(start):
            at = pl.multiple_of(start + base + i * step, LANES)
            return jnp.concatenate([msg[:, pl.ds(at, step)] for msg in msgs], axis=0)

        both = lax.dot_general(left(0), right, TN, preferred_element_type=F32)
        down = lax.dot_general(left(width), hidden, TN, preferred_element_type=F32)
        for k, total in enumerate((both[:, :units], both[:, units:], down)):
            if added:
                total += added[k][rows].astype(F32)
            outs[k][rows] = total.astype(BF)


def shift(value, axis, offset):
    size = lax.axis_size(axis)
    return lax.ppermute(value, axis, [(i, (i + offset) % size) for i in range(size)])


def shift_two(value, offset, column):
    pairs = [
        (4 * i + j, 4 * ((i + offset) % 4) + (j + column) % 4) for i in range(4) for j in range(4)
    ]
    return lax.ppermute(value, ("expert", "y"), pairs)


def exchange(value, axis):
    return lax.all_to_all(value, axis, split_axis=0, concat_axis=0, tiled=True)


def after(value, *others):
    return lax.optimization_barrier((value, *others))[0]


def on_device(tokens, cotangent, gate_weights, expert_ids, w_gate, w_up, w_down):
    tok_count, width = tokens.shape
    slots = tok_count * 3 // 4
    units = w_gate.shape[2]
    block = width // 4
    zs = lax.axis_size("z")
    rows = tok_count // zs
    long = 2 * width + LANES
    pos = jnp.stack(
        [lax.axis_index(name) for name in ("dp", "expert", "z", "y")]
    ).astype(jnp.int32)
    given = (expert_ids.T, gate_weights.T)

    far, tokens, cotangent = call(
        far_kernel,
        [array(slots // 2, width + LANES), array(*tokens.shape), array(*tokens.shape)],
        (pos, *given, tokens, cotangent),
        free=(0, 1, 2, 3),
        unblocked=(2, 3),
        scratch=[pltpu.SemaphoreType.DMA((2,))],
    )
    given = (*given, tokens, cotangent)
    plus, minus = call(
        functools.partial(near_kernel, (1, -1)),
        [array(slots, long)] * 2,
        (pos, *given),
        free=(0, 1),
    )
    then = after(pos, plus)
    (here,) = call(
        functools.partial(near_kernel, (0,)), [array(slots, long)], (then, *given),
        free=(0, 1),
    )
    weights = []
    for own in (w_gate, w_up, w_down):
        weights += [own, shift(after(own, plus), "dp", 1)]
    plus, minus = shift(plus, "expert", 1), shift(minus, "expert", -1)
    far = shift(far, "expert", 2)
    far = [far] + [shift(far, "y", offset) for offset in (1, -1, 2)]

    def expert(pos, msgs, kind):
        count = 2 if kind == "sides" else 1
        return call(
            functools.partial(expert_kernel, kind),
            [array(slots + 8, block)] * (4 * count)
            + [plain(count * slots, 3 * units)]
            + [array(slots, long)] * (kind == "far"),
            (pos, *msgs, *weights),
            scratch=[pltpu.VMEM((4, count * slots, block), BF)],
        )

    def back(sends, offset):
        kept = [sends[0]] if offset == 0 else [shift_two(sends[0], -offset, 0)]
        return kept + [shift_two(sends[j], -offset, j) for j in (1, 3, 2)]

    local = expert(pos, [here], "here")
    remote = expert(after(pos, local[0]), far, "far")
    sides = expert(after(pos, remote[0]), [plus, minus], "sides")
    groups = [*back(local[:4], 0), *back(sides[:4], 1), *back(sides[4:8], -1), *back(remote[:4], 2)]
    (mine,) = call(combine_kernel, [plain(zs, rows, block + LANES)], (pos, expert_ids.T, *groups))
    mine, gate_grad = call(
        gather_kernel,
        [plain(zs, rows, block), plain(2, tok_count)],
        (pos, expert_ids.T, exchange(mine, "z")),
    )
    slab = exchange(mine, "z").reshape(tok_count, block)
    (input_grad,) = call(
        columns_kernel,
        [plain(tok_count, width)],
        (pos, slab, *[shift(slab, "y", offset) for offset in (1, -1, 2)]),
    )
    used = [here, remote[5], plus, minus, local[4], remote[4], sides[8]]
    half = width // 2
    away = call(
        functools.partial(grad_kernel, True), [array(half, units)] * 3, (pos, *used),
        limit=12,
    )
    received = [shift(part, "dp", 1) for part in away]
    grads = call(
        functools.partial(grad_kernel, False), [plain(half, units)] * 3, (pos, *used, *received),
        limit=12,
    )
    return (input_grad, gate_grad.T, grads[0][None], grads[1][None], grads[2][None])


def solution(mesh):
    dp, experts, tensor = (mesh.shape[name] for name in ("dp", "expert", "tensor"))
    view = Mesh(mesh.devices.reshape(dp, experts, tensor // 4, 4), ("dp", "expert", "z", "y"))
    row = P(("dp", "expert"), None)
    weight = P("expert", "dp", ("z", "y"))

    return jax.shard_map(
        on_device,
        mesh=view,
        in_specs=(row, row, row, row, weight, weight, weight),
        out_specs=(row, row, weight, weight, weight),
        check_vma=False,
    )
```

```python
import functools

import jax
import jax.numpy as jnp
from jax import lax
from jax.experimental import pallas as pl
from jax.experimental.pallas import tpu as pltpu
from jax.sharding import Mesh, PartitionSpec as P


BF = jnp.bfloat16
F32 = jnp.float32
NT = (((1,), (1,)), ((), ()))
TN = (((0,), (0,)), ((), ()))
LANES = 128
OFFSETS = (0, 1, -1, 2)


MIB = 1 << 20


def array(*shape):
    return pltpu.VMEM(shape, BF)


def plain(*shape):
    return pltpu.HBM(shape, BF)


def call(kernel, outs, operands, limit=8, scratch=(), free=(), unblocked=()):
    spec = pl.BlockSpec(memory_space=pltpu.VMEM)
    specs = [pl.BlockSpec(memory_space=pltpu.SMEM)]
    kept = [operands[0]]
    for k, value in enumerate(operands[1:]):
        specs.append(pl.BlockSpec(memory_space=pl.ANY) if k in unblocked else spec)
        space = pltpu.HBM if k in free else pltpu.VMEM
        kept.append(pltpu.with_memory_space_constraint(value, space))
    return pl.pallas_call(
        kernel,
        out_shape=outs,
        in_specs=specs,
        out_specs=[spec] * len(outs),
        scratch_shapes=list(scratch),
        compiler_params=pltpu.CompilerParams(vmem_limit_bytes=limit * MIB),
    )(*kept)


def routing(pos, ids_ref, offsets):
    tokens = ids_ref.shape[1]
    ids = ids_ref[...]
    before = (
        lax.broadcasted_iota(jnp.int32, (tokens, tokens), 0)
        < lax.broadcasted_iota(jnp.int32, (tokens, tokens), 1)
    ).astype(BF)
    hits = [ids == lax.rem(pos[1] + offset + 4, 4) for offset in offsets]
    rows = [jnp.max(hit.astype(F32), axis=0, keepdims=True) for hit in hits]
    member = jnp.concatenate(rows + [jnp.zeros((8 - len(rows), tokens), F32)], axis=0)
    rank = jnp.dot(member.astype(BF), before, preferred_element_type=F32)
    return member, rank, hits


def picks(rank, member, j, slots, first):
    slot = lax.broadcasted_iota(jnp.int32, (slots, rank.shape[1]), 0)
    slot = (slot + first).astype(F32)
    hit = (slot == rank[j : j + 1]) & (member[j : j + 1] > 0.5)
    return jnp.where(hit, 1.0, 0.0).astype(BF)


def facts_of(pick, hit, gw_ref):
    tokens = pick.shape[1]
    weight = jnp.sum(jnp.where(hit, gw_ref[...].astype(F32), 0.0), axis=0, keepdims=True)
    facts = jnp.where(lax.broadcasted_iota(jnp.int32, (LANES, tokens), 0) == 0, weight, 0.0)
    return lax.dot_general(pick, facts.astype(BF), NT, preferred_element_type=F32).astype(BF)


def far_kernel(pos, ids_ref, gw_ref, tok_ref, cot_ref, out, tok_out, cot_out, sems):
    copies = [
        pltpu.make_async_copy(tok_ref, tok_out, sems.at[0]),
        pltpu.make_async_copy(cot_ref, cot_out, sems.at[1]),
    ]
    for copy in copies:
        copy.start()
    member, rank, hits = routing(pos, ids_ref, (2,))
    width = tok_ref.shape[1]
    slots = out.shape[0]
    pick = picks(rank, member, 0, slots, lax.rem(pos[3], 2) * slots)
    out[:, width:] = facts_of(pick, hits[0], gw_ref)
    for copy in copies:
        copy.wait()

    @pl.when(pos[3] < 2)
    def _():
        out[:, :width] = jnp.dot(pick, tok_out[...], preferred_element_type=F32).astype(BF)

    @pl.when(pos[3] >= 2)
    def _():
        out[:, :width] = jnp.dot(pick, cot_out[...], preferred_element_type=F32).astype(BF)


def near_kernel(offsets, pos, ids_ref, gw_ref, tok_ref, cot_ref, *outs):
    member, rank, hits = routing(pos, ids_ref, offsets)
    width = tok_ref.shape[1]
    for j, out in enumerate(outs):
        pick = picks(rank, member, j, out.shape[0], 0)
        out[:, :width] = jnp.dot(pick, tok_ref[...], preferred_element_type=F32).astype(BF)
        out[:, width : 2 * width] = jnp.dot(
            pick, cot_ref[...], preferred_element_type=F32
        ).astype(BF)
        out[:, 2 * width :] = facts_of(pick, hits[j], gw_ref)


def expert_kernel(kind, pos, *refs):
    count = {"here": 1, "far": 4, "sides": 2}[kind]
    pieces, refs = refs[:count], refs[count:]
    wg_own, wg_sib, wu_own, wu_sib, wd_own, wd_sib = (ref.at[0] for ref in refs[:6])
    sends, aux_ref, whole = refs[6:10], refs[10], refs[-1]
    half, units = wg_own.shape
    width = 2 * half
    block = half // 2
    if kind == "far":
        msgs = [refs[11]]
        rows = pieces[0].shape[0]
        for piece, shift in zip(pieces, (0, 1, -1, 2)):
            source = lax.rem(pos[3] - shift + 4, 4)
            at = pl.multiple_of(lax.rem(source, 2) * rows, 16)
            column = pl.multiple_of(lax.div(source, 2) * width, LANES)
            msgs[0][pl.ds(at, rows), pl.ds(column, width)] = piece[:, :width]
            msgs[0][pl.ds(at, rows), 2 * width :] = piece[:, width:]
    else:
        msgs = pieces
    own = pl.multiple_of(pos[0] * half, LANES)
    sib = pl.multiple_of((1 - pos[0]) * half, LANES)

    def columns(at, size):
        parts = [msg[:, pl.ds(at, size)] for msg in msgs]
        return parts[0] if len(parts) == 1 else jnp.concatenate(parts, axis=0)

    facts = columns(2 * width, LANES)
    g = facts[:, :1].astype(F32)

    def product(left_own, left_sib, w_own, w_sib):
        left = jnp.dot(left_own, w_own[...], preferred_element_type=F32)
        return left + jnp.dot(left_sib, w_sib[...], preferred_element_type=F32)

    x_own, x_sib = columns(own, half), columns(sib, half)
    gate = product(x_own, x_sib, wg_own, wg_sib)
    up = product(x_own, x_sib, wu_own, wu_sib)
    back = product(columns(width + own, half), columns(width + sib, half), wd_own, wd_sib)
    sig = jax.nn.sigmoid(gate)
    act = gate * sig
    hid = act * up
    share = hid.astype(BF).astype(F32) * back
    hg = g * back
    dpg = (hg * up * sig * (1.0 + gate * (1.0 - sig))).astype(BF)
    dpu = (hg * act).astype(BF)
    aux_ref[:, :units] = dpg
    aux_ref[:, units : 2 * units] = dpu
    aux_ref[:, 2 * units : 3 * units] = (g * hid).astype(BF)
    for j in range(4):
        wg, wu = (wg_own, wu_own) if j < 2 else (wg_sib, wu_sib)
        at = (j % 2) * block
        part = lax.dot_general(dpg, wg[at : at + block, :], NT, preferred_element_type=F32)
        part += lax.dot_general(dpu, wu[at : at + block, :], NT, preferred_element_type=F32)
        whole[j] = part.astype(BF)
    count = len(msgs)
    long = sends[0].shape[0] // count
    slots = long - 8
    for c in range(count):
        at = slice(c * slots, (c + 1) * slots)
        first = c * long
        padded = jnp.concatenate([share[at], jnp.zeros((LANES - slots, units), F32)], axis=0)
        line = lax.dot_general(
            jnp.ones((8, units), F32), padded, NT,
            precision=lax.Precision.HIGHEST, preferred_element_type=F32,
        ).astype(BF)
        for j, send in enumerate(sends):
            send[first : first + slots] = whole[lax.rem(pos[3] + j, 4), at, :]
            send[first + slots : first + long, :LANES] = line
            send[first + slots : first + long, LANES:] = jnp.zeros((8, block - LANES), BF)


def sum_kernel(pos, a_ref, b_ref, c_ref, d_ref, *outs):
    long = outs[0].shape[0]
    for i, out in enumerate(outs):
        at = slice(i * long, (i + 1) * long)
        total = a_ref[at].astype(F32) + b_ref[at].astype(F32)
        out[...] = (total + (c_ref[at].astype(F32) + d_ref[at].astype(F32))).astype(BF)


def combine_kernel(pos, ids_ref, *refs):
    out_ref = refs[-1]
    zs, rows, wide = out_ref.shape
    tokens = zs * rows
    width = wide - LANES
    slots = refs[0].shape[0] - 8
    member, rank, _ = routing(pos, ids_ref, OFFSETS)
    result = jnp.zeros((tokens, width), F32)
    gates = []
    for k in range(4):
        total = refs[k][...]
        pick = picks(rank, member, k, slots, 0)
        result += lax.dot_general(pick, total[:slots], TN, preferred_element_type=F32)
        pick = picks(rank, member, k, LANES, 0)
        line = jnp.dot(total[slots:, :LANES], pick, preferred_element_type=F32)
        gates.append(line[:1])
    gates = jnp.concatenate(gates + [jnp.zeros((rows - 4, tokens), F32)], axis=0).astype(BF)
    result = result.astype(BF)
    for z in range(zs):
        out_ref[z, :, :width] = result[z * rows : (z + 1) * rows]
        out_ref[z, :, width:] = gates


def gather_kernel(pos, ids_ref, got_ref, out_ref, gate_ref):
    width = out_ref.shape[2]
    total = got_ref[0].astype(F32)
    for z in range(1, got_ref.shape[0]):
        total += got_ref[z].astype(F32)
    slab = total[:, :width].astype(BF)
    for z in range(out_ref.shape[0]):
        out_ref[z] = slab
    ids = ids_ref[...]
    gates = jnp.zeros(ids.shape, F32)
    for k, offset in enumerate(OFFSETS):
        hit = ids == lax.rem(pos[1] + offset + 4, 4)
        gates += jnp.where(hit, total[k : k + 1, width:], 0.0)
    gate_ref[...] = gates.astype(BF)


def columns_kernel(pos, *refs):
    pieces, out_ref = refs[:4], refs[4]
    width = pieces[0].shape[1]
    for piece, shift in zip(pieces, (0, 1, -1, 2)):
        block = lax.rem(pos[3] - shift + 4 + 2 * pos[0], 4)
        out_ref[:, pl.ds(pl.multiple_of(block * width, LANES), width)] = piece[...]


def grad_kernel(other, pos, here_ref, far_ref, plus_ref, minus_ref, *refs):
    msgs = (here_ref, far_ref, plus_ref, minus_ref)
    auxs, added, outs = refs[:3], refs[3:-3], refs[-3:]
    half, units = outs[0].shape
    width = 2 * half
    base = ((1 - pos[0]) if other else pos[0]) * half
    step = 256
    right = jnp.concatenate([ref[:, : 2 * units] for ref in auxs], axis=0)
    hidden = jnp.concatenate([ref[:, 2 * units : 3 * units] for ref in auxs], axis=0)
    for i in range(half // step):
        rows = slice(i * step, (i + 1) * step)

        def left(start):
            at = pl.multiple_of(start + base + i * step, LANES)
            return jnp.concatenate([msg[:, pl.ds(at, step)] for msg in msgs], axis=0)

        both = lax.dot_general(left(0), right, TN, preferred_element_type=F32)
        down = lax.dot_general(left(width), hidden, TN, preferred_element_type=F32)
        for k, total in enumerate((both[:, :units], both[:, units:], down)):
            if added:
                total += added[k][rows].astype(F32)
            outs[k][rows] = total.astype(BF)


def shift(value, axis, offset):
    size = lax.axis_size(axis)
    return lax.ppermute(value, axis, [(i, (i + offset) % size) for i in range(size)])


def exchange(value, axis):
    return lax.all_to_all(value, axis, split_axis=0, concat_axis=0, tiled=True)


def after(value, *others):
    return lax.optimization_barrier((value, *others))[0]


def on_device(tokens, cotangent, gate_weights, expert_ids, w_gate, w_up, w_down):
    tok_count, width = tokens.shape
    slots = tok_count * 3 // 4
    units = w_gate.shape[2]
    block = width // 4
    zs = lax.axis_size("z")
    rows = tok_count // zs
    long = 2 * width + LANES
    pos = jnp.stack(
        [lax.axis_index(name) for name in ("dp", "expert", "z", "y")]
    ).astype(jnp.int32)
    given = (expert_ids.T, gate_weights.T)

    far, tokens, cotangent = call(
        far_kernel,
        [array(slots // 2, width + LANES), array(*tokens.shape), array(*tokens.shape)],
        (pos, *given, tokens, cotangent),
        free=(0, 1, 2, 3),
        unblocked=(2, 3),
        scratch=[pltpu.SemaphoreType.DMA((2,))],
    )
    given = (*given, tokens, cotangent)
    plus, minus = call(
        functools.partial(near_kernel, (1, -1)),
        [array(slots, long)] * 2,
        (pos, *given),
        free=(0, 1),
    )
    then = after(pos, plus)
    (here,) = call(
        functools.partial(near_kernel, (0,)), [array(slots, long)], (then, *given),
        free=(0, 1),
    )
    weights = []
    for own in (w_gate, w_up, w_down):
        weights += [own, shift(after(own, plus), "dp", 1)]
    plus, minus = shift(plus, "expert", 1), shift(minus, "expert", -1)
    far = shift(far, "expert", 2)
    far = [far] + [shift(far, "y", offset) for offset in (1, -1, 2)]

    def expert(pos, msgs, kind):
        count = 2 if kind == "sides" else 1
        return call(
            functools.partial(expert_kernel, kind),
            [array(count * (slots + 8), block)] * 4
            + [plain(count * slots, 3 * units)]
            + [array(slots, long)] * (kind == "far"),
            (pos, *msgs, *weights),
            scratch=[pltpu.VMEM((4, count * slots, block), BF)],
        )

    def scatter(sends, name):
        got = [sends[0]] + [shift(sends[j], "y", j) for j in (1, 3, 2)]
        count = 2 if name == "sides" else 1
        return call(sum_kernel, [array(slots + 8, block)] * count, (pos, *got))

    local = expert(pos, [here], "here")
    remote = expert(after(pos, local[0]), far, "far")
    sides = expert(after(pos, remote[0]), [plus, minus], "sides")
    (from_here,) = scatter(local[:4], "here")
    (from_far,) = scatter(remote[:4], "far")
    from_plus, from_minus = scatter(sides[:4], "sides")
    groups = [
        from_here,
        shift(from_plus, "expert", -1),
        shift(from_minus, "expert", 1),
        shift(from_far, "expert", 2),
    ]
    (mine,) = call(combine_kernel, [plain(zs, rows, block + LANES)], (pos, expert_ids.T, *groups))
    mine, gate_grad = call(
        gather_kernel,
        [plain(zs, rows, block), plain(2, tok_count)],
        (pos, expert_ids.T, exchange(mine, "z")),
    )
    slab = exchange(mine, "z").reshape(tok_count, block)
    (input_grad,) = call(
        columns_kernel,
        [plain(tok_count, width)],
        (pos, slab, *[shift(slab, "y", offset) for offset in (1, -1, 2)]),
    )
    used = [here, remote[5], plus, minus, local[4], remote[4], sides[4]]
    half = width // 2
    away = call(
        functools.partial(grad_kernel, True), [array(half, units)] * 3, (pos, *used),
        limit=12,
    )
    received = [shift(part, "dp", 1) for part in away]
    grads = call(
        functools.partial(grad_kernel, False), [plain(half, units)] * 3, (pos, *used, *received),
        limit=12,
    )
    return (input_grad, gate_grad.T, grads[0][None], grads[1][None], grads[2][None])


def solution(mesh):
    dp, experts, tensor = (mesh.shape[name] for name in ("dp", "expert", "tensor"))
    view = Mesh(mesh.devices.reshape(dp, experts, tensor // 4, 4), ("dp", "expert", "z", "y"))
    row = P(("dp", "expert"), None)
    weight = P("expert", "dp", ("z", "y"))

    return jax.shard_map(
        on_device,
        mesh=view,
        in_specs=(row, row, row, row, weight, weight, weight),
        out_specs=(row, row, weight, weight, weight),
        check_vma=False,
    )
```

```python
import functools

import jax
import jax.numpy as jnp
from jax import lax
from jax.experimental import pallas as pl
from jax.experimental.pallas import tpu as pltpu
from jax.sharding import Mesh, PartitionSpec as P


BF = jnp.bfloat16
F32 = jnp.float32
NT = (((1,), (1,)), ((), ()))
TN = (((0,), (0,)), ((), ()))
LANES = 128
OFFSETS = (0, 1, -1, 2)


MIB = 1 << 20


def array(*shape):
    return pltpu.VMEM(shape, BF)


def plain(*shape):
    return pltpu.HBM(shape, BF)


def call(kernel, outs, operands, limit=8, scratch=(), free=(), unblocked=()):
    spec = pl.BlockSpec(memory_space=pltpu.VMEM)
    specs = [pl.BlockSpec(memory_space=pltpu.SMEM)]
    kept = [operands[0]]
    for k, value in enumerate(operands[1:]):
        specs.append(pl.BlockSpec(memory_space=pl.ANY) if k in unblocked else spec)
        space = pltpu.HBM if k in free else pltpu.VMEM
        kept.append(pltpu.with_memory_space_constraint(value, space))
    return pl.pallas_call(
        kernel,
        out_shape=outs,
        in_specs=specs,
        out_specs=[spec] * len(outs),
        scratch_shapes=list(scratch),
        compiler_params=pltpu.CompilerParams(vmem_limit_bytes=limit * MIB),
    )(*kept)


def routing(pos, ids_ref, offsets):
    tokens = ids_ref.shape[1]
    ids = ids_ref[...]
    before = (
        lax.broadcasted_iota(jnp.int32, (tokens, tokens), 0)
        < lax.broadcasted_iota(jnp.int32, (tokens, tokens), 1)
    ).astype(BF)
    hits = [ids == lax.rem(pos[1] + offset + 4, 4) for offset in offsets]
    rows = [jnp.max(hit.astype(F32), axis=0, keepdims=True) for hit in hits]
    member = jnp.concatenate(rows + [jnp.zeros((8 - len(rows), tokens), F32)], axis=0)
    rank = jnp.dot(member.astype(BF), before, preferred_element_type=F32)
    return member, rank, hits


def picks(rank, member, j, slots, first):
    slot = lax.broadcasted_iota(jnp.int32, (slots, rank.shape[1]), 0)
    slot = (slot + first).astype(F32)
    hit = (slot == rank[j : j + 1]) & (member[j : j + 1] > 0.5)
    return jnp.where(hit, 1.0, 0.0).astype(BF)


def facts_of(pick, hit, gw_ref):
    tokens = pick.shape[1]
    weight = jnp.sum(jnp.where(hit, gw_ref[...].astype(F32), 0.0), axis=0, keepdims=True)
    facts = jnp.where(lax.broadcasted_iota(jnp.int32, (LANES, tokens), 0) == 0, weight, 0.0)
    return lax.dot_general(pick, facts.astype(BF), NT, preferred_element_type=F32).astype(BF)


def far_kernel(pos, ids_in, gw_in, tok_ref, cot_ref, out, tok_out, cot_out, ids_ref, gw_ref, sems):
    pairs = ((ids_in, ids_ref), (gw_in, gw_ref), (tok_ref, tok_out), (cot_ref, cot_out))
    copies = [pltpu.make_async_copy(a, b, sems.at[k]) for k, (a, b) in enumerate(pairs)]
    for copy in copies:
        copy.start()
    copies[0].wait()
    copies[1].wait()
    member, rank, hits = routing(pos, ids_ref, (2,))
    width = tok_ref.shape[1]
    slots = out.shape[0]
    pick = picks(rank, member, 0, slots, lax.rem(pos[3], 2) * slots)
    out[:, width:] = facts_of(pick, hits[0], gw_ref)
    copies[2].wait()

    @pl.when(pos[3] < 2)
    def _():
        out[:, :width] = jnp.dot(pick, tok_out[...], preferred_element_type=F32).astype(BF)

    copies[3].wait()

    @pl.when(pos[3] >= 2)
    def _():
        out[:, :width] = jnp.dot(pick, cot_out[...], preferred_element_type=F32).astype(BF)


def near_kernel(offsets, pos, ids_ref, gw_ref, tok_ref, cot_ref, *outs):
    member, rank, hits = routing(pos, ids_ref, offsets)
    width = tok_ref.shape[1]
    for j, out in enumerate(outs):
        pick = picks(rank, member, j, out.shape[0], 0)
        out[:, :width] = jnp.dot(pick, tok_ref[...], preferred_element_type=F32).astype(BF)
        out[:, width : 2 * width] = jnp.dot(
            pick, cot_ref[...], preferred_element_type=F32
        ).astype(BF)
        out[:, 2 * width :] = facts_of(pick, hits[j], gw_ref)


def expert_kernel(kind, pos, *refs):
    count = {"here": 1, "far": 4, "sides": 2}[kind]
    pieces, refs = refs[:count], refs[count:]
    wg_own, wg_sib, wu_own, wu_sib, wd_own, wd_sib = (ref.at[0] for ref in refs[:6])
    ends = 14 if kind == "sides" else 10
    sends, aux_ref, whole = refs[6:ends], refs[ends], refs[-1]
    half, units = wg_own.shape
    width = 2 * half
    block = half // 2
    if kind == "far":
        msgs = [refs[ends + 1]]
        rows = pieces[0].shape[0]
        for piece, shift in zip(pieces, (0, 1, -1, 2)):
            source = lax.rem(pos[3] - shift + 4, 4)
            at = pl.multiple_of(lax.rem(source, 2) * rows, 16)
            column = pl.multiple_of(lax.div(source, 2) * width, LANES)
            msgs[0][pl.ds(at, rows), pl.ds(column, width)] = piece[:, :width]
            msgs[0][pl.ds(at, rows), 2 * width :] = piece[:, width:]
    else:
        msgs = pieces
    own = pl.multiple_of(pos[0] * half, LANES)
    sib = pl.multiple_of((1 - pos[0]) * half, LANES)

    def columns(at, size):
        parts = [msg[:, pl.ds(at, size)] for msg in msgs]
        return parts[0] if len(parts) == 1 else jnp.concatenate(parts, axis=0)

    facts = columns(2 * width, LANES)
    g = facts[:, :1].astype(F32)

    def product(left_own, left_sib, w_own, w_sib):
        left = jnp.dot(left_own, w_own[...], preferred_element_type=F32)
        return left + jnp.dot(left_sib, w_sib[...], preferred_element_type=F32)

    x_own, x_sib = columns(own, half), columns(sib, half)
    gate = product(x_own, x_sib, wg_own, wg_sib)
    up = product(x_own, x_sib, wu_own, wu_sib)
    back = product(columns(width + own, half), columns(width + sib, half), wd_own, wd_sib)
    sig = jax.nn.sigmoid(gate)
    act = gate * sig
    hid = act * up
    share = hid.astype(BF).astype(F32) * back
    hg = g * back
    dpg = (hg * up * sig * (1.0 + gate * (1.0 - sig))).astype(BF)
    dpu = (hg * act).astype(BF)
    aux_ref[:, :units] = dpg
    aux_ref[:, units : 2 * units] = dpu
    aux_ref[:, 2 * units : 3 * units] = (g * hid).astype(BF)
    for j in range(4):
        wg, wu = (wg_own, wu_own) if j < 2 else (wg_sib, wu_sib)
        at = (j % 2) * block
        part = lax.dot_general(dpg, wg[at : at + block, :], NT, preferred_element_type=F32)
        part += lax.dot_general(dpu, wu[at : at + block, :], NT, preferred_element_type=F32)
        whole[j] = part.astype(BF)
    slots = sends[0].shape[0] - 8
    for c in range(len(msgs)):
        at = slice(c * slots, (c + 1) * slots)
        padded = jnp.concatenate([share[at], jnp.zeros((LANES - slots, units), F32)], axis=0)
        line = lax.dot_general(
            jnp.ones((8, units), F32), padded, NT,
            precision=lax.Precision.HIGHEST, preferred_element_type=F32,
        ).astype(BF)
        for j, send in enumerate(sends[4 * c : 4 * c + 4]):
            send[:slots] = whole[lax.rem(pos[3] + j, 4), at, :]
            send[slots:, :LANES] = line
            send[slots:, LANES:] = jnp.zeros((8, block - LANES), BF)


def sum_kernel(pos, a_ref, b_ref, c_ref, d_ref, out):
    total = a_ref[...].astype(F32) + b_ref[...].astype(F32)
    out[...] = (total + (c_ref[...].astype(F32) + d_ref[...].astype(F32))).astype(BF)


def combine_kernel(pos, ids_ref, *refs):
    out_ref = refs[-1]
    zs, rows, wide = out_ref.shape
    tokens = zs * rows
    width = wide - LANES
    slots = refs[0].shape[0] - 8
    groups = (refs[:1], refs[1:5], refs[5:9], refs[9:10])
    member, rank, _ = routing(pos, ids_ref, OFFSETS)
    result = jnp.zeros((tokens, width), F32)
    gates = []
    for k in range(4):
        total = groups[k][0][...]
        if len(groups[k]) > 1:
            total = total.astype(F32)
            for ref in groups[k][1:]:
                total += ref[...].astype(F32)
            total = total.astype(BF)
        pick = picks(rank, member, k, slots, 0)
        result += lax.dot_general(pick, total[:slots], TN, preferred_element_type=F32)
        pick = picks(rank, member, k, LANES, 0)
        line = jnp.dot(total[slots:, :LANES], pick, preferred_element_type=F32)
        gates.append(line[:1])
    gates = jnp.concatenate(gates + [jnp.zeros((rows - 4, tokens), F32)], axis=0).astype(BF)
    result = result.astype(BF)
    for z in range(zs):
        out_ref[z, :, :width] = result[z * rows : (z + 1) * rows]
        out_ref[z, :, width:] = gates


def gather_kernel(pos, ids_ref, got_ref, out_ref, gate_ref):
    width = out_ref.shape[2]
    total = got_ref[0].astype(F32)
    for z in range(1, got_ref.shape[0]):
        total += got_ref[z].astype(F32)
    slab = total[:, :width].astype(BF)
    for z in range(out_ref.shape[0]):
        out_ref[z] = slab
    ids = ids_ref[...]
    gates = jnp.zeros(ids.shape, F32)
    for k, offset in enumerate(OFFSETS):
        hit = ids == lax.rem(pos[1] + offset + 4, 4)
        gates += jnp.where(hit, total[k : k + 1, width:], 0.0)
    gate_ref[...] = gates.astype(BF)


def columns_kernel(pos, *refs):
    pieces, out_ref = refs[:4], refs[4]
    width = pieces[0].shape[1]
    for piece, shift in zip(pieces, (0, 1, -1, 2)):
        block = lax.rem(pos[3] - shift + 4 + 2 * pos[0], 4)
        out_ref[:, pl.ds(pl.multiple_of(block * width, LANES), width)] = piece[...]


def grad_kernel(other, pos, here_ref, far_ref, plus_ref, minus_ref, *refs):
    msgs = (here_ref, far_ref, plus_ref, minus_ref)
    auxs, added, outs = refs[:3], refs[3:-3], refs[-3:]
    half, units = outs[0].shape
    width = 2 * half
    base = ((1 - pos[0]) if other else pos[0]) * half
    step = 256
    right = jnp.concatenate([ref[:, : 2 * units] for ref in auxs], axis=0)
    hidden = jnp.concatenate([ref[:, 2 * units : 3 * units] for ref in auxs], axis=0)
    for i in range(half // step):
        rows = slice(i * step, (i + 1) * step)

        def left(start):
            at = pl.multiple_of(start + base + i * step, LANES)
            return jnp.concatenate([msg[:, pl.ds(at, step)] for msg in msgs], axis=0)

        both = lax.dot_general(left(0), right, TN, preferred_element_type=F32)
        down = lax.dot_general(left(width), hidden, TN, preferred_element_type=F32)
        for k, total in enumerate((both[:, :units], both[:, units:], down)):
            if added:
                total += added[k][rows].astype(F32)
            outs[k][rows] = total.astype(BF)


def shift(value, axis, offset):
    size = lax.axis_size(axis)
    return lax.ppermute(value, axis, [(i, (i + offset) % size) for i in range(size)])


def shift_two(value, offset, column):
    pairs = [
        (4 * i + j, 4 * ((i + offset) % 4) + (j + column) % 4) for i in range(4) for j in range(4)
    ]
    return lax.ppermute(value, ("expert", "y"), pairs)


def exchange(value, axis):
    return lax.all_to_all(value, axis, split_axis=0, concat_axis=0, tiled=True)


def after(value, *others):
    return lax.optimization_barrier((value, *others))[0]


def on_device(tokens, cotangent, gate_weights, expert_ids, w_gate, w_up, w_down):
    tok_count, width = tokens.shape
    slots = tok_count * 3 // 4
    units = w_gate.shape[2]
    block = width // 4
    zs = lax.axis_size("z")
    rows = tok_count // zs
    long = 2 * width + LANES
    pos = jnp.stack(
        [lax.axis_index(name) for name in ("dp", "expert", "z", "y")]
    ).astype(jnp.int32)
    given = (expert_ids.T, gate_weights.T)

    far, tokens, cotangent = call(
        far_kernel,
        [array(slots // 2, width + LANES), array(*tokens.shape), array(*tokens.shape)],
        (pos, *given, tokens, cotangent),
        free=(0, 1, 2, 3),
        unblocked=(0, 1, 2, 3),
        scratch=[
            pltpu.VMEM(given[0].shape, jnp.int32),
            pltpu.VMEM(given[1].shape, BF),
            pltpu.SemaphoreType.DMA((4,)),
        ],
    )
    given = (*given, tokens, cotangent)
    plus, minus = call(
        functools.partial(near_kernel, (1, -1)),
        [array(slots, long)] * 2,
        (pos, *given),
        free=(0, 1),
    )
    then = after(pos, plus)
    (here,) = call(
        functools.partial(near_kernel, (0,)), [array(slots, long)], (then, *given),
        free=(0, 1),
    )
    weights = []
    for own in (w_gate, w_up, w_down):
        weights += [own, shift(after(own, plus), "dp", 1)]
    plus, minus = shift(plus, "expert", 1), shift(minus, "expert", -1)
    far = shift(far, "expert", 2)
    far = [far] + [shift(far, "y", offset) for offset in (1, -1, 2)]

    def expert(pos, msgs, kind):
        count = 2 if kind == "sides" else 1
        return call(
            functools.partial(expert_kernel, kind),
            [array(slots + 8, block)] * (4 * count)
            + [array(count * slots, 3 * units)]
            + [array(slots, long)] * (kind == "far"),
            (pos, *msgs, *weights),
            scratch=[pltpu.VMEM((4, count * slots, block), BF)],
        )

    def scatter(sends):
        got = [sends[0]] + [shift(sends[j], "y", j) for j in (1, 3, 2)]
        return call(sum_kernel, [array(slots + 8, block)], (pos, *got))[0]

    def direct(sends, offset):
        return [shift_two(sends[j], -offset, j) for j in (2, 1, 3, 0)]

    local = expert(pos, [here], "here")
    remote = expert(after(pos, local[0]), far, "far")
    sides = expert(after(pos, remote[0]), [plus, minus], "sides")
    groups = [
        scatter(local[:4]),
        *direct(sides[:4], 1),
        *direct(sides[4:8], -1),
        shift(scatter(remote[:4]), "expert", 2),
    ]
    (mine,) = call(combine_kernel, [plain(zs, rows, block + LANES)], (pos, expert_ids.T, *groups))
    mine, gate_grad = call(
        gather_kernel,
        [plain(zs, rows, block), plain(2, tok_count)],
        (pos, expert_ids.T, exchange(mine, "z")),
    )
    slab = exchange(mine, "z").reshape(tok_count, block)
    (input_grad,) = call(
        columns_kernel,
        [plain(tok_count, width)],
        (pos, slab, *[shift(slab, "y", offset) for offset in (1, -1, 2)]),
    )
    used = [here, remote[5], plus, minus, local[4], remote[4], sides[8]]
    half = width // 2
    away = call(
        functools.partial(grad_kernel, True), [array(half, units)] * 3, (pos, *used),
        limit=12,
    )
    received = [shift(part, "dp", 1) for part in away]
    grads = call(
        functools.partial(grad_kernel, False), [plain(half, units)] * 3, (pos, *used, *received),
        limit=12,
    )
    return (input_grad, gate_grad.T, grads[0][None], grads[1][None], grads[2][None])


def solution(mesh):
    dp, experts, tensor = (mesh.shape[name] for name in ("dp", "expert", "tensor"))
    view = Mesh(mesh.devices.reshape(dp, experts, tensor // 4, 4), ("dp", "expert", "z", "y"))
    row = P(("dp", "expert"), None)
    weight = P("expert", "dp", ("z", "y"))

    return jax.shard_map(
        on_device,
        mesh=view,
        in_specs=(row, row, row, row, weight, weight, weight),
        out_specs=(row, row, weight, weight, weight),
        check_vma=False,
    )
```

```python
import functools

import jax
import jax.numpy as jnp
from jax import lax
from jax.experimental import pallas as pl
from jax.experimental.pallas import tpu as pltpu
from jax.sharding import Mesh, PartitionSpec as P


BF = jnp.bfloat16
F32 = jnp.float32
NT = (((1,), (1,)), ((), ()))
TN = (((0,), (0,)), ((), ()))
LANES = 128
OFFSETS = (0, 1, -1, 2)


MIB = 1 << 20


def array(*shape):
    return pltpu.VMEM(shape, BF)


def plain(*shape):
    return pltpu.HBM(shape, BF)


def call(kernel, outs, operands, limit=8, scratch=(), free=(), unblocked=()):
    spec = pl.BlockSpec(memory_space=pltpu.VMEM)
    specs = [pl.BlockSpec(memory_space=pltpu.SMEM)]
    kept = [operands[0]]
    for k, value in enumerate(operands[1:]):
        specs.append(pl.BlockSpec(memory_space=pl.ANY) if k in unblocked else spec)
        space = pltpu.HBM if k in free else pltpu.VMEM
        kept.append(pltpu.with_memory_space_constraint(value, space))
    return pl.pallas_call(
        kernel,
        out_shape=outs,
        in_specs=specs,
        out_specs=[spec] * len(outs),
        scratch_shapes=list(scratch),
        compiler_params=pltpu.CompilerParams(vmem_limit_bytes=limit * MIB),
    )(*kept)


def routing(pos, ids_ref, offsets):
    tokens = ids_ref.shape[1]
    ids = ids_ref[...]
    before = (
        lax.broadcasted_iota(jnp.int32, (tokens, tokens), 0)
        < lax.broadcasted_iota(jnp.int32, (tokens, tokens), 1)
    ).astype(BF)
    hits = [ids == lax.rem(pos[1] + offset + 4, 4) for offset in offsets]
    rows = [jnp.max(hit.astype(F32), axis=0, keepdims=True) for hit in hits]
    member = jnp.concatenate(rows + [jnp.zeros((8 - len(rows), tokens), F32)], axis=0)
    rank = jnp.dot(member.astype(BF), before, preferred_element_type=F32)
    return member, rank, hits


def picks(rank, member, j, slots, first):
    slot = lax.broadcasted_iota(jnp.int32, (slots, rank.shape[1]), 0)
    slot = (slot + first).astype(F32)
    hit = (slot == rank[j : j + 1]) & (member[j : j + 1] > 0.5)
    return jnp.where(hit, 1.0, 0.0).astype(BF)


def facts_of(pick, hit, gw_ref):
    tokens = pick.shape[1]
    weight = jnp.sum(jnp.where(hit, gw_ref[...].astype(F32), 0.0), axis=0, keepdims=True)
    facts = jnp.where(lax.broadcasted_iota(jnp.int32, (LANES, tokens), 0) == 0, weight, 0.0)
    return lax.dot_general(pick, facts.astype(BF), NT, preferred_element_type=F32).astype(BF)


def far_kernel(pos, ids_in, gw_in, tok_ref, cot_ref, out, tok_out, cot_out, ids_ref, gw_ref, sems):
    pairs = ((ids_in, ids_ref), (gw_in, gw_ref), (tok_ref, tok_out), (cot_ref, cot_out))
    copies = [pltpu.make_async_copy(a, b, sems.at[k]) for k, (a, b) in enumerate(pairs)]
    for copy in copies:
        copy.start()
    copies[0].wait()
    copies[1].wait()
    member, rank, hits = routing(pos, ids_ref, (2,))
    width = tok_ref.shape[1]
    slots = out.shape[0]
    pick = picks(rank, member, 0, slots, lax.rem(pos[3], 2) * slots)
    out[:, width:] = facts_of(pick, hits[0], gw_ref)
    copies[2].wait()

    @pl.when(pos[3] < 2)
    def _():
        out[:, :width] = jnp.dot(pick, tok_out[...], preferred_element_type=F32).astype(BF)

    copies[3].wait()

    @pl.when(pos[3] >= 2)
    def _():
        out[:, :width] = jnp.dot(pick, cot_out[...], preferred_element_type=F32).astype(BF)


def near_kernel(offsets, pos, ids_ref, gw_ref, tok_ref, cot_ref, *outs):
    member, rank, hits = routing(pos, ids_ref, offsets)
    width = tok_ref.shape[1]
    for j, out in enumerate(outs):
        pick = picks(rank, member, j, out.shape[0], 0)
        out[:, :width] = jnp.dot(pick, tok_ref[...], preferred_element_type=F32).astype(BF)
        out[:, width : 2 * width] = jnp.dot(
            pick, cot_ref[...], preferred_element_type=F32
        ).astype(BF)
        out[:, 2 * width :] = facts_of(pick, hits[j], gw_ref)


def expert_kernel(kind, pos, *refs):
    count = {"here": 1, "far": 4, "sides": 2}[kind]
    pieces, refs = refs[:count], refs[count:]
    wg_own, wg_sib, wu_own, wu_sib, wd_own, wd_sib = (ref.at[0] for ref in refs[:6])
    sends, aux_ref, whole = refs[6:10], refs[10], refs[-1]
    half, units = wg_own.shape
    width = 2 * half
    block = half // 2
    if kind == "far":
        msgs = [refs[11]]
        rows = pieces[0].shape[0]
        for piece, shift in zip(pieces, (0, 1, -1, 2)):
            source = lax.rem(pos[3] - shift + 4, 4)
            at = pl.multiple_of(lax.rem(source, 2) * rows, 16)
            column = pl.multiple_of(lax.div(source, 2) * width, LANES)
            msgs[0][pl.ds(at, rows), pl.ds(column, width)] = piece[:, :width]
            msgs[0][pl.ds(at, rows), 2 * width :] = piece[:, width:]
    else:
        msgs = pieces
    own = pl.multiple_of(pos[0] * half, LANES)
    sib = pl.multiple_of((1 - pos[0]) * half, LANES)

    def columns(at, size):
        parts = [msg[:, pl.ds(at, size)] for msg in msgs]
        return parts[0] if len(parts) == 1 else jnp.concatenate(parts, axis=0)

    facts = columns(2 * width, LANES)
    g = facts[:, :1].astype(F32)

    def product(left_own, left_sib, w_own, w_sib):
        left = jnp.dot(left_own, w_own[...], preferred_element_type=F32)
        return left + jnp.dot(left_sib, w_sib[...], preferred_element_type=F32)

    x_own, x_sib = columns(own, half), columns(sib, half)
    gate = product(x_own, x_sib, wg_own, wg_sib)
    up = product(x_own, x_sib, wu_own, wu_sib)
    back = product(columns(width + own, half), columns(width + sib, half), wd_own, wd_sib)
    sig = jax.nn.sigmoid(gate)
    act = gate * sig
    hid = act * up
    share = hid.astype(BF).astype(F32) * back
    hg = g * back
    dpg = (hg * up * sig * (1.0 + gate * (1.0 - sig))).astype(BF)
    dpu = (hg * act).astype(BF)
    aux_ref[:, :units] = dpg
    aux_ref[:, units : 2 * units] = dpu
    aux_ref[:, 2 * units : 3 * units] = (g * hid).astype(BF)
    for j in range(4):
        wg, wu = (wg_own, wu_own) if j < 2 else (wg_sib, wu_sib)
        at = (j % 2) * block
        part = lax.dot_general(dpg, wg[at : at + block, :], NT, preferred_element_type=F32)
        part += lax.dot_general(dpu, wu[at : at + block, :], NT, preferred_element_type=F32)
        whole[j] = part.astype(BF)
    count = len(msgs)
    long = sends[0].shape[0] // count
    slots = long - 8
    for c in range(count):
        at = slice(c * slots, (c + 1) * slots)
        first = c * long
        padded = jnp.concatenate([share[at], jnp.zeros((LANES - slots, units), F32)], axis=0)
        line = lax.dot_general(
            jnp.ones((8, units), F32), padded, NT,
            precision=lax.Precision.HIGHEST, preferred_element_type=F32,
        ).astype(BF)
        for j, send in enumerate(sends):
            send[first : first + slots] = whole[lax.rem(pos[3] + j, 4), at, :]
            send[first + slots : first + long, :LANES] = line
            send[first + slots : first + long, LANES:] = jnp.zeros((8, block - LANES), BF)


def sum_kernel(pos, a_ref, b_ref, c_ref, d_ref, *outs):
    long = outs[0].shape[0]
    for i, out in enumerate(outs):
        at = slice(i * long, (i + 1) * long)
        total = a_ref[at].astype(F32) + b_ref[at].astype(F32)
        out[...] = (total + (c_ref[at].astype(F32) + d_ref[at].astype(F32))).astype(BF)


def combine_kernel(pos, ids_ref, *refs):
    out_ref = refs[-1]
    zs, rows, wide = out_ref.shape
    tokens = zs * rows
    width = wide - LANES
    slots = refs[0].shape[0] - 8
    member, rank, _ = routing(pos, ids_ref, OFFSETS)
    result = jnp.zeros((tokens, width), F32)
    gates = []
    for k in range(4):
        total = refs[k][...]
        pick = picks(rank, member, k, slots, 0)
        result += lax.dot_general(pick, total[:slots], TN, preferred_element_type=F32)
        pick = picks(rank, member, k, LANES, 0)
        line = jnp.dot(total[slots:, :LANES], pick, preferred_element_type=F32)
        gates.append(line[:1])
    gates = jnp.concatenate(gates + [jnp.zeros((rows - 4, tokens), F32)], axis=0).astype(BF)
    result = result.astype(BF)
    for z in range(zs):
        out_ref[z, :, :width] = result[z * rows : (z + 1) * rows]
        out_ref[z, :, width:] = gates


def gather_kernel(pos, ids_ref, got_ref, out_ref, gate_ref):
    width = out_ref.shape[2]
    total = got_ref[0].astype(F32)
    for z in range(1, got_ref.shape[0]):
        total += got_ref[z].astype(F32)
    slab = total[:, :width].astype(BF)
    for z in range(out_ref.shape[0]):
        out_ref[z] = slab
    ids = ids_ref[...]
    gates = jnp.zeros(ids.shape, F32)
    for k, offset in enumerate(OFFSETS):
        hit = ids == lax.rem(pos[1] + offset + 4, 4)
        gates += jnp.where(hit, total[k : k + 1, width:], 0.0)
    gate_ref[...] = gates.astype(BF)


def columns_kernel(pos, *refs):
    pieces, out_ref = refs[:4], refs[4]
    width = pieces[0].shape[1]
    for piece, shift in zip(pieces, (0, 1, -1, 2)):
        block = lax.rem(pos[3] - shift + 4 + 2 * pos[0], 4)
        out_ref[:, pl.ds(pl.multiple_of(block * width, LANES), width)] = piece[...]


def grad_kernel(other, pos, here_ref, far_ref, plus_ref, minus_ref, *refs):
    msgs = (here_ref, far_ref, plus_ref, minus_ref)
    auxs, added, outs = refs[:3], refs[3:-3], refs[-3:]
    half, units = outs[0].shape
    width = 2 * half
    base = ((1 - pos[0]) if other else pos[0]) * half
    step = 256
    right = jnp.concatenate([ref[:, : 2 * units] for ref in auxs], axis=0)
    hidden = jnp.concatenate([ref[:, 2 * units : 3 * units] for ref in auxs], axis=0)
    for i in range(half // step):
        rows = slice(i * step, (i + 1) * step)

        def left(start):
            at = pl.multiple_of(start + base + i * step, LANES)
            return jnp.concatenate([msg[:, pl.ds(at, step)] for msg in msgs], axis=0)

        both = lax.dot_general(left(0), right, TN, preferred_element_type=F32)
        down = lax.dot_general(left(width), hidden, TN, preferred_element_type=F32)
        for k, total in enumerate((both[:, :units], both[:, units:], down)):
            if added:
                total += added[k][rows].astype(F32)
            outs[k][rows] = total.astype(BF)


def shift(value, axis, offset):
    size = lax.axis_size(axis)
    return lax.ppermute(value, axis, [(i, (i + offset) % size) for i in range(size)])


def exchange(value, axis):
    return lax.all_to_all(value, axis, split_axis=0, concat_axis=0, tiled=True)


def after(value, *others):
    return lax.optimization_barrier((value, *others))[0]


def on_device(tokens, cotangent, gate_weights, expert_ids, w_gate, w_up, w_down):
    tok_count, width = tokens.shape
    slots = tok_count * 3 // 4
    units = w_gate.shape[2]
    block = width // 4
    zs = lax.axis_size("z")
    rows = tok_count // zs
    long = 2 * width + LANES
    pos = jnp.stack(
        [lax.axis_index(name) for name in ("dp", "expert", "z", "y")]
    ).astype(jnp.int32)
    given = (expert_ids.T, gate_weights.T)

    far, tokens, cotangent = call(
        far_kernel,
        [array(slots // 2, width + LANES), array(*tokens.shape), array(*tokens.shape)],
        (pos, *given, tokens, cotangent),
        free=(0, 1, 2, 3),
        unblocked=(0, 1, 2, 3),
        scratch=[
            pltpu.VMEM(given[0].shape, jnp.int32),
            pltpu.VMEM(given[1].shape, BF),
            pltpu.SemaphoreType.DMA((4,)),
        ],
    )
    given = (*given, tokens, cotangent)
    plus, minus = call(
        functools.partial(near_kernel, (1, -1)),
        [array(slots, long)] * 2,
        (pos, *given),
        free=(0, 1),
    )
    then = after(pos, plus)
    (here,) = call(
        functools.partial(near_kernel, (0,)), [array(slots, long)], (then, *given),
        free=(0, 1),
    )
    weights = []
    for own in (w_gate, w_up, w_down):
        weights += [own, shift(after(own, plus), "dp", 1)]
    plus, minus = shift(plus, "expert", 1), shift(minus, "expert", -1)
    far = shift(far, "expert", 2)
    far = [far] + [shift(far, "y", offset) for offset in (1, -1, 2)]

    def expert(pos, msgs, kind):
        count = 2 if kind == "sides" else 1
        return call(
            functools.partial(expert_kernel, kind),
            [array(count * (slots + 8), block)] * 4
            + [array(count * slots, 3 * units)]
            + [array(slots, long)] * (kind == "far"),
            (pos, *msgs, *weights),
            scratch=[pltpu.VMEM((4, count * slots, block), BF)],
        )

    def scatter(sends, name):
        got = [sends[0]] + [shift(sends[j], "y", j) for j in (1, 3, 2)]
        count = 2 if name == "sides" else 1
        return call(sum_kernel, [array(slots + 8, block)] * count, (pos, *got))

    local = expert(pos, [here], "here")
    remote = expert(after(pos, local[0]), far, "far")
    sides = expert(after(pos, remote[0]), [plus, minus], "sides")
    (from_here,) = scatter(local[:4], "here")
    (from_far,) = scatter(remote[:4], "far")
    from_plus, from_minus = scatter(sides[:4], "sides")
    groups = [
        from_here,
        shift(from_plus, "expert", -1),
        shift(from_minus, "expert", 1),
        shift(from_far, "expert", 2),
    ]
    (mine,) = call(combine_kernel, [plain(zs, rows, block + LANES)], (pos, expert_ids.T, *groups))
    mine, gate_grad = call(
        gather_kernel,
        [plain(zs, rows, block), plain(2, tok_count)],
        (pos, expert_ids.T, exchange(mine, "z")),
    )
    slab = exchange(mine, "z").reshape(tok_count, block)
    (input_grad,) = call(
        columns_kernel,
        [plain(tok_count, width)],
        (pos, slab, *[shift(slab, "y", offset) for offset in (1, -1, 2)]),
    )
    used = [here, remote[5], plus, minus, local[4], remote[4], sides[4]]
    half = width // 2
    away = call(
        functools.partial(grad_kernel, True), [array(half, units)] * 3, (pos, *used),
        limit=12,
    )
    received = [shift(part, "dp", 1) for part in away]
    grads = call(
        functools.partial(grad_kernel, False), [plain(half, units)] * 3, (pos, *used, *received),
        limit=12,
    )
    return (input_grad, gate_grad.T, grads[0][None], grads[1][None], grads[2][None])


def solution(mesh):
    dp, experts, tensor = (mesh.shape[name] for name in ("dp", "expert", "tensor"))
    view = Mesh(mesh.devices.reshape(dp, experts, tensor // 4, 4), ("dp", "expert", "z", "y"))
    row = P(("dp", "expert"), None)
    weight = P("expert", "dp", ("z", "y"))

    return jax.shard_map(
        on_device,
        mesh=view,
        in_specs=(row, row, row, row, weight, weight, weight),
        out_specs=(row, row, weight, weight, weight),
        check_vma=False,
    )
```

```python
import functools

import jax
import jax.numpy as jnp
from jax import lax
from jax.experimental import pallas as pl
from jax.experimental.pallas import tpu as pltpu
from jax.sharding import Mesh, PartitionSpec as P


BF = jnp.bfloat16
F32 = jnp.float32
NT = (((1,), (1,)), ((), ()))
TN = (((0,), (0,)), ((), ()))
LANES = 128
OFFSETS = (0, 1, -1, 2)


MIB = 1 << 20


def array(*shape):
    return pltpu.VMEM(shape, BF)


def plain(*shape):
    return pltpu.HBM(shape, BF)


def call(kernel, outs, operands, limit=8, scratch=(), free=(), unblocked=()):
    spec = pl.BlockSpec(memory_space=pltpu.VMEM)
    specs = [pl.BlockSpec(memory_space=pltpu.SMEM)]
    kept = [operands[0]]
    for k, value in enumerate(operands[1:]):
        specs.append(pl.BlockSpec(memory_space=pl.ANY) if k in unblocked else spec)
        space = pltpu.HBM if k in free else pltpu.VMEM
        kept.append(pltpu.with_memory_space_constraint(value, space))
    return pl.pallas_call(
        kernel,
        out_shape=outs,
        in_specs=specs,
        out_specs=[spec] * len(outs),
        scratch_shapes=list(scratch),
        compiler_params=pltpu.CompilerParams(vmem_limit_bytes=limit * MIB),
    )(*kept)


def routing(pos, ids_ref, offsets):
    tokens = ids_ref.shape[1]
    ids = ids_ref[...]
    before = (
        lax.broadcasted_iota(jnp.int32, (tokens, tokens), 0)
        < lax.broadcasted_iota(jnp.int32, (tokens, tokens), 1)
    ).astype(BF)
    hits = [ids == lax.rem(pos[1] + offset + 4, 4) for offset in offsets]
    rows = [jnp.max(hit.astype(F32), axis=0, keepdims=True) for hit in hits]
    member = jnp.concatenate(rows + [jnp.zeros((8 - len(rows), tokens), F32)], axis=0)
    rank = jnp.dot(member.astype(BF), before, preferred_element_type=F32)
    return member, rank, hits


def picks(rank, member, j, slots, first):
    slot = lax.broadcasted_iota(jnp.int32, (slots, rank.shape[1]), 0)
    slot = (slot + first).astype(F32)
    hit = (slot == rank[j : j + 1]) & (member[j : j + 1] > 0.5)
    return jnp.where(hit, 1.0, 0.0).astype(BF)


def facts_of(pick, hit, gw_ref):
    tokens = pick.shape[1]
    weight = jnp.sum(jnp.where(hit, gw_ref[...].astype(F32), 0.0), axis=0, keepdims=True)
    facts = jnp.where(lax.broadcasted_iota(jnp.int32, (LANES, tokens), 0) == 0, weight, 0.0)
    return lax.dot_general(pick, facts.astype(BF), NT, preferred_element_type=F32).astype(BF)


def far_kernel(pos, ids_in, gw_in, tok_ref, cot_ref, out, tok_out, cot_out, ids_ref, gw_ref, sems):
    pairs = ((ids_in, ids_ref), (gw_in, gw_ref), (tok_ref, tok_out), (cot_ref, cot_out))
    copies = [pltpu.make_async_copy(a, b, sems.at[k]) for k, (a, b) in enumerate(pairs)]
    for copy in copies:
        copy.start()
    copies[0].wait()
    copies[1].wait()
    member, rank, hits = routing(pos, ids_ref, (2,))
    width = tok_ref.shape[1]
    slots = out.shape[0]
    pick = picks(rank, member, 0, slots, lax.rem(pos[3], 2) * slots)
    out[:, width:] = facts_of(pick, hits[0], gw_ref)
    copies[2].wait()

    @pl.when(pos[3] < 2)
    def _():
        out[:, :width] = jnp.dot(pick, tok_out[...], preferred_element_type=F32).astype(BF)

    copies[3].wait()

    @pl.when(pos[3] >= 2)
    def _():
        out[:, :width] = jnp.dot(pick, cot_out[...], preferred_element_type=F32).astype(BF)


def near_kernel(offsets, pos, ids_ref, gw_ref, tok_ref, cot_ref, *outs):
    member, rank, hits = routing(pos, ids_ref, offsets)
    width = tok_ref.shape[1]
    for j, out in enumerate(outs):
        pick = picks(rank, member, j, out.shape[0], 0)
        out[:, :width] = jnp.dot(pick, tok_ref[...], preferred_element_type=F32).astype(BF)
        out[:, width : 2 * width] = jnp.dot(
            pick, cot_ref[...], preferred_element_type=F32
        ).astype(BF)
        out[:, 2 * width :] = facts_of(pick, hits[j], gw_ref)


def here_kernel(pos, ids_ref, gw_ref, tok_ref, cot_ref, out, picks_ref):
    near_kernel((0,), pos, ids_ref, gw_ref, tok_ref, cot_ref, out)
    member, rank, _ = routing(pos, ids_ref, OFFSETS)
    for k in range(4):
        picks_ref[k] = picks(rank, member, k, picks_ref.shape[1], 0)


def expert_kernel(kind, pos, *refs):
    count = {"here": 1, "far": 4, "sides": 2}[kind]
    pieces, refs = refs[:count], refs[count:]
    wg_own, wg_sib, wu_own, wu_sib, wd_own, wd_sib = (ref.at[0] for ref in refs[:6])
    sends, aux_ref, whole = refs[6:10], refs[10], refs[-1]
    half, units = wg_own.shape
    width = 2 * half
    block = half // 2
    if kind == "far":
        msgs = [refs[11]]
        rows = pieces[0].shape[0]
        for piece, shift in zip(pieces, (0, 1, -1, 2)):
            source = lax.rem(pos[3] - shift + 4, 4)
            at = pl.multiple_of(lax.rem(source, 2) * rows, 16)
            column = pl.multiple_of(lax.div(source, 2) * width, LANES)
            msgs[0][pl.ds(at, rows), pl.ds(column, width)] = piece[:, :width]
            msgs[0][pl.ds(at, rows), 2 * width :] = piece[:, width:]
    else:
        msgs = pieces
    own = pl.multiple_of(pos[0] * half, LANES)
    sib = pl.multiple_of((1 - pos[0]) * half, LANES)

    def columns(at, size):
        parts = [msg[:, pl.ds(at, size)] for msg in msgs]
        return parts[0] if len(parts) == 1 else jnp.concatenate(parts, axis=0)

    facts = columns(2 * width, LANES)
    g = facts[:, :1].astype(F32)

    def product(left_own, left_sib, w_own, w_sib):
        left = jnp.dot(left_own, w_own[...], preferred_element_type=F32)
        return left + jnp.dot(left_sib, w_sib[...], preferred_element_type=F32)

    x_own, x_sib = columns(own, half), columns(sib, half)
    gate = product(x_own, x_sib, wg_own, wg_sib)
    up = product(x_own, x_sib, wu_own, wu_sib)
    back = product(columns(width + own, half), columns(width + sib, half), wd_own, wd_sib)
    sig = jax.nn.sigmoid(gate)
    act = gate * sig
    hid = act * up
    share = hid.astype(BF).astype(F32) * back
    hg = g * back
    dpg = (hg * up * sig * (1.0 + gate * (1.0 - sig))).astype(BF)
    dpu = (hg * act).astype(BF)
    aux_ref[:, :units] = dpg
    aux_ref[:, units : 2 * units] = dpu
    aux_ref[:, 2 * units : 3 * units] = (g * hid).astype(BF)
    for j in range(4):
        wg, wu = (wg_own, wu_own) if j < 2 else (wg_sib, wu_sib)
        at = (j % 2) * block
        part = lax.dot_general(dpg, wg[at : at + block, :], NT, preferred_element_type=F32)
        part += lax.dot_general(dpu, wu[at : at + block, :], NT, preferred_element_type=F32)
        whole[j] = part.astype(BF)
    count = len(msgs)
    long = sends[0].shape[0] // count
    slots = long - 8
    for c in range(count):
        at = slice(c * slots, (c + 1) * slots)
        first = c * long
        padded = jnp.concatenate([share[at], jnp.zeros((LANES - slots, units), F32)], axis=0)
        line = lax.dot_general(
            jnp.ones((8, units), F32), padded, NT,
            precision=lax.Precision.HIGHEST, preferred_element_type=F32,
        ).astype(BF)
        for j, send in enumerate(sends):
            send[first : first + slots] = whole[lax.rem(pos[3] + j, 4), at, :]
            send[first + slots : first + long, :LANES] = line
            send[first + slots : first + long, LANES:] = jnp.zeros((8, block - LANES), BF)


def sum_kernel(pos, a_ref, b_ref, c_ref, d_ref, *outs):
    long = outs[0].shape[0]
    for i, out in enumerate(outs):
        at = slice(i * long, (i + 1) * long)
        total = a_ref[at].astype(F32) + b_ref[at].astype(F32)
        out[...] = (total + (c_ref[at].astype(F32) + d_ref[at].astype(F32))).astype(BF)


def combine_kernel(pos, picks_ref, *refs):
    out_ref = refs[-1]
    zs, rows, wide = out_ref.shape
    tokens = zs * rows
    width = wide - LANES
    slots = refs[0].shape[0] - 8
    result = jnp.zeros((tokens, width), F32)
    gates = []
    for k in range(4):
        total = refs[k][...]
        pick = picks_ref[k, :slots]
        result += lax.dot_general(pick, total[:slots], TN, preferred_element_type=F32)
        line = jnp.dot(total[slots:, :LANES], picks_ref[k], preferred_element_type=F32)
        gates.append(line[:1])
    gates = jnp.concatenate(gates + [jnp.zeros((rows - 4, tokens), F32)], axis=0).astype(BF)
    result = result.astype(BF)
    for z in range(zs):
        out_ref[z, :, :width] = result[z * rows : (z + 1) * rows]
        out_ref[z, :, width:] = gates


def gather_kernel(pos, ids_ref, got_ref, out_ref, gate_ref):
    width = out_ref.shape[2]
    total = got_ref[0].astype(F32)
    for z in range(1, got_ref.shape[0]):
        total += got_ref[z].astype(F32)
    slab = total[:, :width].astype(BF)
    for z in range(out_ref.shape[0]):
        out_ref[z] = slab
    ids = ids_ref[...]
    gates = jnp.zeros(ids.shape, F32)
    for k, offset in enumerate(OFFSETS):
        hit = ids == lax.rem(pos[1] + offset + 4, 4)
        gates += jnp.where(hit, total[k : k + 1, width:], 0.0)
    gate_ref[...] = gates.astype(BF)


def columns_kernel(pos, *refs):
    pieces, out_ref = refs[:4], refs[4]
    width = pieces[0].shape[1]
    for piece, shift in zip(pieces, (0, 1, -1, 2)):
        block = lax.rem(pos[3] - shift + 4 + 2 * pos[0], 4)
        out_ref[:, pl.ds(pl.multiple_of(block * width, LANES), width)] = piece[...]


def grad_kernel(other, pos, here_ref, far_ref, plus_ref, minus_ref, *refs):
    msgs = (here_ref, far_ref, plus_ref, minus_ref)
    auxs, added, outs = refs[:3], refs[3:-3], refs[-3:]
    half, units = outs[0].shape
    width = 2 * half
    base = ((1 - pos[0]) if other else pos[0]) * half
    step = 256
    right = jnp.concatenate([ref[:, : 2 * units] for ref in auxs], axis=0)
    hidden = jnp.concatenate([ref[:, 2 * units : 3 * units] for ref in auxs], axis=0)
    for i in range(half // step):
        rows = slice(i * step, (i + 1) * step)

        def left(start):
            at = pl.multiple_of(start + base + i * step, LANES)
            return jnp.concatenate([msg[:, pl.ds(at, step)] for msg in msgs], axis=0)

        both = lax.dot_general(left(0), right, TN, preferred_element_type=F32)
        down = lax.dot_general(left(width), hidden, TN, preferred_element_type=F32)
        for k, total in enumerate((both[:, :units], both[:, units:], down)):
            if added:
                total += added[k][rows].astype(F32)
            outs[k][rows] = total.astype(BF)


def shift(value, axis, offset):
    size = lax.axis_size(axis)
    return lax.ppermute(value, axis, [(i, (i + offset) % size) for i in range(size)])


def exchange(value, axis):
    return lax.all_to_all(value, axis, split_axis=0, concat_axis=0, tiled=True)


def after(value, *others):
    return lax.optimization_barrier((value, *others))[0]


def on_device(tokens, cotangent, gate_weights, expert_ids, w_gate, w_up, w_down):
    tok_count, width = tokens.shape
    slots = tok_count * 3 // 4
    units = w_gate.shape[2]
    block = width // 4
    zs = lax.axis_size("z")
    rows = tok_count // zs
    long = 2 * width + LANES
    pos = jnp.stack(
        [lax.axis_index(name) for name in ("dp", "expert", "z", "y")]
    ).astype(jnp.int32)
    given = (expert_ids.T, gate_weights.T)

    far, tokens, cotangent = call(
        far_kernel,
        [array(slots // 2, width + LANES), array(*tokens.shape), array(*tokens.shape)],
        (pos, *given, tokens, cotangent),
        free=(0, 1, 2, 3),
        unblocked=(0, 1, 2, 3),
        scratch=[
            pltpu.VMEM(given[0].shape, jnp.int32),
            pltpu.VMEM(given[1].shape, BF),
            pltpu.SemaphoreType.DMA((4,)),
        ],
    )
    given = (*given, tokens, cotangent)
    plus, minus = call(
        functools.partial(near_kernel, (1, -1)),
        [array(slots, long)] * 2,
        (pos, *given),
        free=(0, 1),
    )
    then = after(pos, plus)
    here, chosen = call(
        here_kernel, [array(slots, long), array(4, LANES, tok_count)], (then, *given), free=(0, 1)
    )
    weights = []
    for own in (w_gate, w_up, w_down):
        weights += [own, shift(after(own, plus), "dp", 1)]
    plus, minus = shift(plus, "expert", 1), shift(minus, "expert", -1)
    far = shift(far, "expert", 2)
    far = [far] + [shift(far, "y", offset) for offset in (1, -1, 2)]

    def expert(pos, msgs, kind):
        count = 2 if kind == "sides" else 1
        return call(
            functools.partial(expert_kernel, kind),
            [array(count * (slots + 8), block)] * 4
            + [array(count * slots, 3 * units)]
            + [array(slots, long)] * (kind == "far"),
            (pos, *msgs, *weights),
            scratch=[pltpu.VMEM((4, count * slots, block), BF)],
        )

    def scatter(sends, name):
        got = [sends[0]] + [shift(sends[j], "y", j) for j in (1, 3, 2)]
        count = 2 if name == "sides" else 1
        return call(sum_kernel, [array(slots + 8, block)] * count, (pos, *got))

    local = expert(pos, [here], "here")
    remote = expert(after(pos, local[0]), far, "far")
    sides = expert(after(pos, remote[0]), [plus, minus], "sides")
    (from_here,) = scatter(local[:4], "here")
    (from_far,) = scatter(remote[:4], "far")
    from_plus, from_minus = scatter(sides[:4], "sides")
    groups = [
        from_here,
        shift(from_plus, "expert", -1),
        shift(from_minus, "expert", 1),
        shift(from_far, "expert", 2),
    ]
    (mine,) = call(combine_kernel, [array(zs, rows, block + LANES)], (pos, chosen, *groups))
    mine, gate_grad = call(
        gather_kernel,
        [array(zs, rows, block), plain(2, tok_count)],
        (pos, expert_ids.T, exchange(mine, "z")),
    )
    slab = exchange(mine, "z").reshape(tok_count, block)
    (input_grad,) = call(
        columns_kernel,
        [plain(tok_count, width)],
        (pos, slab, *[shift(slab, "y", offset) for offset in (1, -1, 2)]),
    )
    used = [here, remote[5], plus, minus, local[4], remote[4], sides[4]]
    half = width // 2
    away = call(
        functools.partial(grad_kernel, True), [array(half, units)] * 3, (pos, *used),
        limit=12,
    )
    received = [shift(part, "dp", 1) for part in away]
    grads = call(
        functools.partial(grad_kernel, False), [plain(half, units)] * 3, (pos, *used, *received),
        limit=12,
    )
    return (input_grad, gate_grad.T, grads[0][None], grads[1][None], grads[2][None])


def solution(mesh):
    dp, experts, tensor = (mesh.shape[name] for name in ("dp", "expert", "tensor"))
    view = Mesh(mesh.devices.reshape(dp, experts, tensor // 4, 4), ("dp", "expert", "z", "y"))
    row = P(("dp", "expert"), None)
    weight = P("expert", "dp", ("z", "y"))

    return jax.shard_map(
        on_device,
        mesh=view,
        in_specs=(row, row, row, row, weight, weight, weight),
        out_specs=(row, row, weight, weight, weight),
        check_vma=False,
    )
```

```python
import functools

import jax
import jax.numpy as jnp
from jax import lax
from jax.experimental import pallas as pl
from jax.experimental.pallas import tpu as pltpu
from jax.sharding import Mesh, PartitionSpec as P


BF = jnp.bfloat16
F32 = jnp.float32
NT = (((1,), (1,)), ((), ()))
TN = (((0,), (0,)), ((), ()))
LANES = 128
OFFSETS = (0, 1, -1, 2)


MIB = 1 << 20


def array(*shape):
    return pltpu.VMEM(shape, BF)


def plain(*shape):
    return pltpu.HBM(shape, BF)


def call(kernel, outs, operands, limit=8, scratch=(), free=(), unblocked=()):
    spec = pl.BlockSpec(memory_space=pltpu.VMEM)
    specs = [pl.BlockSpec(memory_space=pltpu.SMEM)]
    kept = [operands[0]]
    for k, value in enumerate(operands[1:]):
        specs.append(pl.BlockSpec(memory_space=pl.ANY) if k in unblocked else spec)
        space = pltpu.HBM if k in free else pltpu.VMEM
        kept.append(pltpu.with_memory_space_constraint(value, space))
    return pl.pallas_call(
        kernel,
        out_shape=outs,
        in_specs=specs,
        out_specs=[spec] * len(outs),
        scratch_shapes=list(scratch),
        compiler_params=pltpu.CompilerParams(vmem_limit_bytes=limit * MIB),
    )(*kept)


def routing(pos, ids_ref, offsets):
    tokens = ids_ref.shape[1]
    ids = ids_ref[...]
    before = (
        lax.broadcasted_iota(jnp.int32, (tokens, tokens), 0)
        < lax.broadcasted_iota(jnp.int32, (tokens, tokens), 1)
    ).astype(BF)
    hits = [ids == lax.rem(pos[1] + offset + 4, 4) for offset in offsets]
    rows = [jnp.max(hit.astype(F32), axis=0, keepdims=True) for hit in hits]
    member = jnp.concatenate(rows + [jnp.zeros((8 - len(rows), tokens), F32)], axis=0)
    rank = jnp.dot(member.astype(BF), before, preferred_element_type=F32)
    return member, rank, hits


def picks(rank, member, j, slots, first):
    slot = lax.broadcasted_iota(jnp.int32, (slots, rank.shape[1]), 0)
    slot = (slot + first).astype(F32)
    hit = (slot == rank[j : j + 1]) & (member[j : j + 1] > 0.5)
    return jnp.where(hit, 1.0, 0.0).astype(BF)


def facts_of(pick, hit, gw_ref):
    tokens = pick.shape[1]
    weight = jnp.sum(jnp.where(hit, gw_ref[...].astype(F32), 0.0), axis=0, keepdims=True)
    facts = jnp.where(lax.broadcasted_iota(jnp.int32, (LANES, tokens), 0) == 0, weight, 0.0)
    return lax.dot_general(pick, facts.astype(BF), NT, preferred_element_type=F32).astype(BF)


def far_kernel(pos, ids_in, gw_in, tok_ref, cot_ref, out, tok_out, cot_out, ids_ref, gw_ref, sems):
    pairs = ((ids_in, ids_ref), (gw_in, gw_ref), (tok_ref, tok_out), (cot_ref, cot_out))
    copies = [pltpu.make_async_copy(a, b, sems.at[k]) for k, (a, b) in enumerate(pairs)]
    for copy in copies:
        copy.start()
    copies[0].wait()
    copies[1].wait()
    member, rank, hits = routing(pos, ids_ref, (2,))
    width = tok_ref.shape[1]
    slots = out.shape[0]
    pick = picks(rank, member, 0, slots, lax.rem(pos[3], 2) * slots)
    out[:, width:] = facts_of(pick, hits[0], gw_ref)
    copies[2].wait()

    @pl.when(pos[3] < 2)
    def _():
        out[:, :width] = jnp.dot(pick, tok_out[...], preferred_element_type=F32).astype(BF)

    copies[3].wait()

    @pl.when(pos[3] >= 2)
    def _():
        out[:, :width] = jnp.dot(pick, cot_out[...], preferred_element_type=F32).astype(BF)


def near_kernel(offsets, pos, ids_ref, gw_ref, tok_ref, cot_ref, *outs):
    member, rank, hits = routing(pos, ids_ref, offsets)
    width = tok_ref.shape[1]
    for j, out in enumerate(outs):
        pick = picks(rank, member, j, out.shape[0], 0)
        out[:, :width] = jnp.dot(pick, tok_ref[...], preferred_element_type=F32).astype(BF)
        out[:, width : 2 * width] = jnp.dot(
            pick, cot_ref[...], preferred_element_type=F32
        ).astype(BF)
        out[:, 2 * width :] = facts_of(pick, hits[j], gw_ref)


def sides_kernel(pos, ids_ref, gw_ref, tok_ref, cot_ref, *outs):
    member, rank, hits = routing(pos, ids_ref, (1, -1))
    width = tok_ref.shape[1]
    half, part = width // 2, width // 4
    at = pl.multiple_of(half + lax.rem(pos[2], 2) * part, LANES)
    for j in range(2):
        out, piece = outs[j], outs[2 + j]
        pick = picks(rank, member, j, out.shape[0], 0)
        piece[...] = jnp.dot(
            pick, cot_ref[:, pl.ds(at, part)], preferred_element_type=F32
        ).astype(BF)
        out[:, :width] = jnp.dot(pick, tok_ref[...], preferred_element_type=F32).astype(BF)
        out[:, width : width + half] = jnp.dot(
            pick, cot_ref[:, :half], preferred_element_type=F32
        ).astype(BF)
        out[:, width + half :] = facts_of(pick, hits[j], gw_ref)


def here_kernel(pos, ids_ref, gw_ref, tok_ref, cot_ref, out, picks_ref):
    near_kernel((0,), pos, ids_ref, gw_ref, tok_ref, cot_ref, out)
    member, rank, _ = routing(pos, ids_ref, OFFSETS)
    for k in range(4):
        picks_ref[k] = picks(rank, member, k, picks_ref.shape[1], 0)


def expert_kernel(kind, pos, *refs):
    count = {"here": 1, "far": 4, "sides": 6}[kind]
    pieces, refs = refs[:count], refs[count:]
    wg_own, wg_sib, wu_own, wu_sib, wd_own, wd_sib = (ref.at[0] for ref in refs[:6])
    sends, aux_ref, whole = refs[6:10], refs[10], refs[-1]
    half, units = wg_own.shape
    width = 2 * half
    block = half // 2
    if kind == "far":
        msgs = [refs[11]]
        rows = pieces[0].shape[0]
        for piece, shift in zip(pieces, (0, 1, -1, 2)):
            source = lax.rem(pos[3] - shift + 4, 4)
            at = pl.multiple_of(lax.rem(source, 2) * rows, 16)
            column = pl.multiple_of(lax.div(source, 2) * width, LANES)
            msgs[0][pl.ds(at, rows), pl.ds(column, width)] = piece[:, :width]
            msgs[0][pl.ds(at, rows), 2 * width :] = piece[:, width:]
    elif kind == "sides":
        msgs = refs[11:13]
        part = half // 2
        first = lax.rem(pos[2], 2)
        ours = pl.multiple_of(width + half + first * part, LANES)
        theirs = pl.multiple_of(width + half + (1 - first) * part, LANES)
        for j, msg in enumerate(msgs):
            main = pieces[j]
            msg[:, : width + half] = main[:, : width + half]
            msg[:, 2 * width :] = main[:, width + half :]
            msg[:, pl.ds(ours, part)] = pieces[2 + j][...]
            msg[:, pl.ds(theirs, part)] = pieces[4 + j][...]
    else:
        msgs = pieces
    own = pl.multiple_of(pos[0] * half, LANES)
    sib = pl.multiple_of((1 - pos[0]) * half, LANES)

    def columns(at, size):
        parts = [msg[:, pl.ds(at, size)] for msg in msgs]
        return parts[0] if len(parts) == 1 else jnp.concatenate(parts, axis=0)

    facts = columns(2 * width, LANES)
    g = facts[:, :1].astype(F32)

    def product(left_own, left_sib, w_own, w_sib):
        left = jnp.dot(left_own, w_own[...], preferred_element_type=F32)
        return left + jnp.dot(left_sib, w_sib[...], preferred_element_type=F32)

    x_own, x_sib = columns(own, half), columns(sib, half)
    gate = product(x_own, x_sib, wg_own, wg_sib)
    up = product(x_own, x_sib, wu_own, wu_sib)
    back = product(columns(width + own, half), columns(width + sib, half), wd_own, wd_sib)
    sig = jax.nn.sigmoid(gate)
    act = gate * sig
    hid = act * up
    share = hid.astype(BF).astype(F32) * back
    hg = g * back
    dpg = (hg * up * sig * (1.0 + gate * (1.0 - sig))).astype(BF)
    dpu = (hg * act).astype(BF)
    aux_ref[:, :units] = dpg
    aux_ref[:, units : 2 * units] = dpu
    aux_ref[:, 2 * units : 3 * units] = (g * hid).astype(BF)
    for j in range(4):
        wg, wu = (wg_own, wu_own) if j < 2 else (wg_sib, wu_sib)
        at = (j % 2) * block
        part = lax.dot_general(dpg, wg[at : at + block, :], NT, preferred_element_type=F32)
        part += lax.dot_general(dpu, wu[at : at + block, :], NT, preferred_element_type=F32)
        whole[j] = part.astype(BF)
    count = len(msgs)
    long = sends[0].shape[0] // count
    slots = long - 8
    for c in range(count):
        at = slice(c * slots, (c + 1) * slots)
        first = c * long
        padded = jnp.concatenate([share[at], jnp.zeros((LANES - slots, units), F32)], axis=0)
        line = lax.dot_general(
            jnp.ones((8, units), F32), padded, NT,
            precision=lax.Precision.HIGHEST, preferred_element_type=F32,
        ).astype(BF)
        for j, send in enumerate(sends):
            send[first : first + slots] = whole[lax.rem(pos[3] + j, 4), at, :]
            send[first + slots : first + long, :LANES] = line
            send[first + slots : first + long, LANES:] = jnp.zeros((8, block - LANES), BF)


def sum_kernel(pos, a_ref, b_ref, c_ref, d_ref, *outs):
    long = outs[0].shape[0]
    for i, out in enumerate(outs):
        at = slice(i * long, (i + 1) * long)
        total = a_ref[at].astype(F32) + b_ref[at].astype(F32)
        out[...] = (total + (c_ref[at].astype(F32) + d_ref[at].astype(F32))).astype(BF)


def combine_kernel(pos, picks_ref, *refs):
    out_ref = refs[-1]
    zs, rows, wide = out_ref.shape
    tokens = zs * rows
    width = wide - LANES
    slots = refs[0].shape[0] - 8
    result = jnp.zeros((tokens, width), F32)
    gates = []
    for k in range(4):
        total = refs[k][...]
        pick = picks_ref[k, :slots]
        result += lax.dot_general(pick, total[:slots], TN, preferred_element_type=F32)
        line = jnp.dot(total[slots:, :LANES], picks_ref[k], preferred_element_type=F32)
        gates.append(line[:1])
    gates = jnp.concatenate(gates + [jnp.zeros((rows - 4, tokens), F32)], axis=0).astype(BF)
    result = result.astype(BF)
    for z in range(zs):
        out_ref[z, :, :width] = result[z * rows : (z + 1) * rows]
        out_ref[z, :, width:] = gates


def gather_kernel(pos, ids_ref, got_ref, out_ref, gate_ref):
    width = out_ref.shape[2]
    total = got_ref[0].astype(F32)
    for z in range(1, got_ref.shape[0]):
        total += got_ref[z].astype(F32)
    slab = total[:, :width].astype(BF)
    for z in range(out_ref.shape[0]):
        out_ref[z] = slab
    ids = ids_ref[...]
    gates = jnp.zeros(ids.shape, F32)
    for k, offset in enumerate(OFFSETS):
        hit = ids == lax.rem(pos[1] + offset + 4, 4)
        gates += jnp.where(hit, total[k : k + 1, width:], 0.0)
    gate_ref[...] = gates.astype(BF)


def columns_kernel(pos, *refs):
    pieces, out_ref = refs[:4], refs[4]
    width = pieces[0].shape[1]
    for piece, shift in zip(pieces, (0, 1, -1, 2)):
        block = lax.rem(pos[3] - shift + 4 + 2 * pos[0], 4)
        out_ref[:, pl.ds(pl.multiple_of(block * width, LANES), width)] = piece[...]


def grad_kernel(other, pos, here_ref, far_ref, plus_ref, minus_ref, *refs):
    msgs = (here_ref, far_ref, plus_ref, minus_ref)
    auxs, added, outs = refs[:3], refs[3:-3], refs[-3:]
    half, units = outs[0].shape
    width = 2 * half
    base = ((1 - pos[0]) if other else pos[0]) * half
    step = 256
    right = jnp.concatenate([ref[:, : 2 * units] for ref in auxs], axis=0)
    hidden = jnp.concatenate([ref[:, 2 * units : 3 * units] for ref in auxs], axis=0)
    for i in range(half // step):
        rows = slice(i * step, (i + 1) * step)

        def left(start):
            at = pl.multiple_of(start + base + i * step, LANES)
            return jnp.concatenate([msg[:, pl.ds(at, step)] for msg in msgs], axis=0)

        both = lax.dot_general(left(0), right, TN, preferred_element_type=F32)
        down = lax.dot_general(left(width), hidden, TN, preferred_element_type=F32)
        for k, total in enumerate((both[:, :units], both[:, units:], down)):
            if added:
                total += added[k][rows].astype(F32)
            outs[k][rows] = total.astype(BF)


def shift(value, axis, offset):
    size = lax.axis_size(axis)
    return lax.ppermute(value, axis, [(i, (i + offset) % size) for i in range(size)])


def swap(value):
    size = lax.axis_size("z")
    return lax.ppermute(value, "z", [(i, i ^ 1) for i in range(size)])


def exchange(value, axis):
    return lax.all_to_all(value, axis, split_axis=0, concat_axis=0, tiled=True)


def after(value, *others):
    return lax.optimization_barrier((value, *others))[0]


def on_device(tokens, cotangent, gate_weights, expert_ids, w_gate, w_up, w_down):
    tok_count, width = tokens.shape
    slots = tok_count * 3 // 4
    units = w_gate.shape[2]
    block = width // 4
    zs = lax.axis_size("z")
    rows = tok_count // zs
    long = 2 * width + LANES
    pos = jnp.stack(
        [lax.axis_index(name) for name in ("dp", "expert", "z", "y")]
    ).astype(jnp.int32)
    given = (expert_ids.T, gate_weights.T)

    far, tokens, cotangent = call(
        far_kernel,
        [array(slots // 2, width + LANES), array(*tokens.shape), array(*tokens.shape)],
        (pos, *given, tokens, cotangent),
        free=(0, 1, 2, 3),
        unblocked=(0, 1, 2, 3),
        scratch=[
            pltpu.VMEM(given[0].shape, jnp.int32),
            pltpu.VMEM(given[1].shape, BF),
            pltpu.SemaphoreType.DMA((4,)),
        ],
    )
    given = (*given, tokens, cotangent)
    part = width // 4
    plus, minus, plus_part, minus_part = call(
        sides_kernel,
        [array(slots, long - 2 * part)] * 2 + [array(slots, part)] * 2,
        (pos, *given),
        free=(0, 1),
    )
    then = after(pos, plus)
    here, chosen = call(
        here_kernel, [array(slots, long), array(4, LANES, tok_count)], (then, *given), free=(0, 1)
    )
    weights = []
    for own in (w_gate, w_up, w_down):
        weights += [own, shift(after(own, plus), "dp", 1)]
    plus_part = shift(plus_part, "expert", 1)
    minus_part = shift(minus_part, "expert", -1)
    plus, minus = shift(plus, "expert", 1), shift(minus, "expert", -1)
    sides_in = [plus, minus, plus_part, minus_part, swap(plus_part), swap(minus_part)]
    far = shift(far, "expert", 2)
    far = [far] + [shift(far, "y", offset) for offset in (1, -1, 2)]

    def expert(pos, msgs, kind):
        count = 2 if kind == "sides" else 1
        return call(
            functools.partial(expert_kernel, kind),
            [array(count * (slots + 8), block)] * 4
            + [array(count * slots, 3 * units)]
            + [array(slots, long)] * {"here": 0, "far": 1, "sides": 2}[kind],
            (pos, *msgs, *weights),
            scratch=[pltpu.VMEM((4, count * slots, block), BF)],
        )

    def scatter(sends, name):
        got = [sends[0]] + [shift(sends[j], "y", j) for j in (1, 3, 2)]
        count = 2 if name == "sides" else 1
        return call(sum_kernel, [array(slots + 8, block)] * count, (pos, *got))

    local = expert(pos, [here], "here")
    remote = expert(after(pos, local[0]), far, "far")
    sides = expert(after(pos, remote[0]), sides_in, "sides")
    (from_here,) = scatter(local[:4], "here")
    (from_far,) = scatter(remote[:4], "far")
    from_plus, from_minus = scatter(sides[:4], "sides")
    groups = [
        from_here,
        shift(from_plus, "expert", -1),
        shift(from_minus, "expert", 1),
        shift(from_far, "expert", 2),
    ]
    (mine,) = call(combine_kernel, [array(zs, rows, block + LANES)], (pos, chosen, *groups))
    mine, gate_grad = call(
        gather_kernel,
        [array(zs, rows, block), plain(2, tok_count)],
        (pos, expert_ids.T, exchange(mine, "z")),
    )
    slab = exchange(mine, "z").reshape(tok_count, block)
    (input_grad,) = call(
        columns_kernel,
        [plain(tok_count, width)],
        (pos, slab, *[shift(slab, "y", offset) for offset in (1, -1, 2)]),
    )
    used = [here, remote[5], sides[5], sides[6], local[4], remote[4], sides[4]]
    half = width // 2
    away = call(
        functools.partial(grad_kernel, True), [array(half, units)] * 3, (pos, *used),
        limit=12,
    )
    received = [shift(part, "dp", 1) for part in away]
    grads = call(
        functools.partial(grad_kernel, False), [plain(half, units)] * 3, (pos, *used, *received),
        limit=12,
    )
    return (input_grad, gate_grad.T, grads[0][None], grads[1][None], grads[2][None])


def solution(mesh):
    dp, experts, tensor = (mesh.shape[name] for name in ("dp", "expert", "tensor"))
    view = Mesh(mesh.devices.reshape(dp, experts, tensor // 4, 4), ("dp", "expert", "z", "y"))
    row = P(("dp", "expert"), None)
    weight = P("expert", "dp", ("z", "y"))

    return jax.shard_map(
        on_device,
        mesh=view,
        in_specs=(row, row, row, row, weight, weight, weight),
        out_specs=(row, row, weight, weight, weight),
        check_vma=False,
    )
```

```python
import functools

import jax
import jax.numpy as jnp
from jax import lax
from jax.experimental import pallas as pl
from jax.experimental.pallas import tpu as pltpu
from jax.sharding import Mesh, PartitionSpec as P


BF = jnp.bfloat16
F32 = jnp.float32
NT = (((1,), (1,)), ((), ()))
TN = (((0,), (0,)), ((), ()))
LANES = 128
OFFSETS = (0, 1, -1, 2)


MIB = 1 << 20


def array(*shape):
    return pltpu.VMEM(shape, BF)


def plain(*shape):
    return pltpu.HBM(shape, BF)


def call(kernel, outs, operands, limit=8, scratch=(), free=(), unblocked=(), out=None):
    spec = pl.BlockSpec(memory_space=pltpu.VMEM)
    specs = [pl.BlockSpec(memory_space=pltpu.SMEM)]
    kept = [operands[0]]
    for k, value in enumerate(operands[1:]):
        specs.append(pl.BlockSpec(memory_space=pl.ANY) if k in unblocked else spec)
        space = pltpu.HBM if k in free else pltpu.VMEM
        kept.append(pltpu.with_memory_space_constraint(value, space))
    return pl.pallas_call(
        kernel,
        out_shape=outs,
        in_specs=specs,
        out_specs=[out or spec] * len(outs),
        scratch_shapes=list(scratch),
        compiler_params=pltpu.CompilerParams(vmem_limit_bytes=limit * MIB),
    )(*kept)


def routing(pos, ids_ref, offsets):
    tokens = ids_ref.shape[1]
    ids = ids_ref[...]
    before = (
        lax.broadcasted_iota(jnp.int32, (tokens, tokens), 0)
        < lax.broadcasted_iota(jnp.int32, (tokens, tokens), 1)
    ).astype(BF)
    hits = [ids == lax.rem(pos[1] + offset + 4, 4) for offset in offsets]
    rows = [jnp.max(hit.astype(F32), axis=0, keepdims=True) for hit in hits]
    member = jnp.concatenate(rows + [jnp.zeros((8 - len(rows), tokens), F32)], axis=0)
    rank = jnp.dot(member.astype(BF), before, preferred_element_type=F32)
    return member, rank, hits


def picks(rank, member, j, slots, first):
    slot = lax.broadcasted_iota(jnp.int32, (slots, rank.shape[1]), 0)
    slot = (slot + first).astype(F32)
    hit = (slot == rank[j : j + 1]) & (member[j : j + 1] > 0.5)
    return jnp.where(hit, 1.0, 0.0).astype(BF)


def facts_of(pick, hit, gw_ref):
    tokens = pick.shape[1]
    weight = jnp.sum(jnp.where(hit, gw_ref[...].astype(F32), 0.0), axis=0, keepdims=True)
    facts = jnp.where(lax.broadcasted_iota(jnp.int32, (LANES, tokens), 0) == 0, weight, 0.0)
    return lax.dot_general(pick, facts.astype(BF), NT, preferred_element_type=F32).astype(BF)


def far_kernel(pos, ids_in, gw_in, tok_ref, cot_ref, out, tok_out, cot_out, ids_ref, gw_ref, sems):
    pairs = ((ids_in, ids_ref), (gw_in, gw_ref), (tok_ref, tok_out), (cot_ref, cot_out))
    copies = [pltpu.make_async_copy(a, b, sems.at[k]) for k, (a, b) in enumerate(pairs)]
    for copy in copies:
        copy.start()
    copies[0].wait()
    copies[1].wait()
    member, rank, hits = routing(pos, ids_ref, (2,))
    width = tok_ref.shape[1]
    slots = out.shape[0]
    pick = picks(rank, member, 0, slots, lax.rem(pos[3], 2) * slots)
    out[:, width:] = facts_of(pick, hits[0], gw_ref)
    copies[2].wait()

    @pl.when(pos[3] < 2)
    def _():
        out[:, :width] = jnp.dot(pick, tok_out[...], preferred_element_type=F32).astype(BF)

    copies[3].wait()

    @pl.when(pos[3] >= 2)
    def _():
        out[:, :width] = jnp.dot(pick, cot_out[...], preferred_element_type=F32).astype(BF)


def near_kernel(offsets, pos, ids_ref, gw_ref, tok_ref, cot_ref, *outs):
    member, rank, hits = routing(pos, ids_ref, offsets)
    width = tok_ref.shape[1]
    for j, out in enumerate(outs):
        pick = picks(rank, member, j, out.shape[0], 0)
        out[:, :width] = jnp.dot(pick, tok_ref[...], preferred_element_type=F32).astype(BF)
        out[:, width : 2 * width] = jnp.dot(
            pick, cot_ref[...], preferred_element_type=F32
        ).astype(BF)
        out[:, 2 * width :] = facts_of(pick, hits[j], gw_ref)


def sides_kernel(pos, ids_ref, gw_ref, tok_ref, cot_ref, *outs):
    member, rank, hits = routing(pos, ids_ref, (1, -1))
    width = tok_ref.shape[1]
    half, part = width // 2, width // 4
    at = pl.multiple_of(half + lax.rem(pos[2], 2) * part, LANES)
    for j in range(2):
        out, piece = outs[j], outs[2 + j]
        pick = picks(rank, member, j, out.shape[0], 0)
        piece[...] = jnp.dot(
            pick, cot_ref[:, pl.ds(at, part)], preferred_element_type=F32
        ).astype(BF)
        out[:, :width] = jnp.dot(pick, tok_ref[...], preferred_element_type=F32).astype(BF)
        out[:, width : width + half] = jnp.dot(
            pick, cot_ref[:, :half], preferred_element_type=F32
        ).astype(BF)
        out[:, width + half :] = facts_of(pick, hits[j], gw_ref)


def here_kernel(pos, ids_ref, gw_ref, tok_ref, cot_ref, out, picks_ref):
    near_kernel((0,), pos, ids_ref, gw_ref, tok_ref, cot_ref, out)
    member, rank, _ = routing(pos, ids_ref, OFFSETS)
    for k in range(4):
        picks_ref[k] = picks(rank, member, k, picks_ref.shape[1], 0)


def expert_kernel(kind, pos, *refs):
    count = {"here": 1, "far": 4, "sides": 6}[kind]
    pieces, refs = refs[:count], refs[count:]
    wg_own, wg_sib, wu_own, wu_sib, wd_own, wd_sib = (ref.at[0] for ref in refs[:6])
    sends, aux_ref, whole = refs[6:10], refs[10], refs[-1]
    half, units = wg_own.shape
    width = 2 * half
    block = half // 2
    if kind == "far":
        msgs = [refs[11]]
        rows = pieces[0].shape[0]
        for piece, shift in zip(pieces, (0, 1, -1, 2)):
            source = lax.rem(pos[3] - shift + 4, 4)
            at = pl.multiple_of(lax.rem(source, 2) * rows, 16)
            column = pl.multiple_of(lax.div(source, 2) * width, LANES)
            msgs[0][pl.ds(at, rows), pl.ds(column, width)] = piece[:, :width]
            msgs[0][pl.ds(at, rows), 2 * width :] = piece[:, width:]
    elif kind == "sides":
        msgs = refs[11:13]
        part = half // 2
        first = lax.rem(pos[2], 2)
        ours = pl.multiple_of(width + half + first * part, LANES)
        theirs = pl.multiple_of(width + half + (1 - first) * part, LANES)
        for j, msg in enumerate(msgs):
            main = pieces[j]
            msg[:, : width + half] = main[:, : width + half]
            msg[:, 2 * width :] = main[:, width + half :]
            msg[:, pl.ds(ours, part)] = pieces[2 + j][...]
            msg[:, pl.ds(theirs, part)] = pieces[4 + j][...]
    else:
        msgs = pieces
    own = pl.multiple_of(pos[0] * half, LANES)
    sib = pl.multiple_of((1 - pos[0]) * half, LANES)

    def columns(at, size):
        parts = [msg[:, pl.ds(at, size)] for msg in msgs]
        return parts[0] if len(parts) == 1 else jnp.concatenate(parts, axis=0)

    facts = columns(2 * width, LANES)
    g = facts[:, :1].astype(F32)

    def product(left_own, left_sib, w_own, w_sib):
        left = jnp.dot(left_own, w_own[...], preferred_element_type=F32)
        return left + jnp.dot(left_sib, w_sib[...], preferred_element_type=F32)

    x_own, x_sib = columns(own, half), columns(sib, half)
    gate = product(x_own, x_sib, wg_own, wg_sib)
    up = product(x_own, x_sib, wu_own, wu_sib)
    back = product(columns(width + own, half), columns(width + sib, half), wd_own, wd_sib)
    sig = jax.nn.sigmoid(gate)
    act = gate * sig
    hid = act * up
    share = hid.astype(BF).astype(F32) * back
    hg = g * back
    dpg = (hg * up * sig * (1.0 + gate * (1.0 - sig))).astype(BF)
    dpu = (hg * act).astype(BF)
    aux_ref[:, :units] = dpg
    aux_ref[:, units : 2 * units] = dpu
    aux_ref[:, 2 * units : 3 * units] = (g * hid).astype(BF)
    for j in range(4):
        wg, wu = (wg_own, wu_own) if j < 2 else (wg_sib, wu_sib)
        at = (j % 2) * block
        part = lax.dot_general(dpg, wg[at : at + block, :], NT, preferred_element_type=F32)
        part += lax.dot_general(dpu, wu[at : at + block, :], NT, preferred_element_type=F32)
        whole[j] = part.astype(BF)
    count = len(msgs)
    long = sends[0].shape[0] // count
    slots = long - 8
    for c in range(count):
        at = slice(c * slots, (c + 1) * slots)
        first = c * long
        padded = jnp.concatenate([share[at], jnp.zeros((LANES - slots, units), F32)], axis=0)
        line = lax.dot_general(
            jnp.ones((8, units), F32), padded, NT,
            precision=lax.Precision.HIGHEST, preferred_element_type=F32,
        ).astype(BF)
        for j, send in enumerate(sends):
            send[first : first + slots] = whole[lax.rem(pos[3] + j, 4), at, :]
            send[first + slots : first + long, :LANES] = line
            send[first + slots : first + long, LANES:] = jnp.zeros((8, block - LANES), BF)


def sum_kernel(pos, a_ref, b_ref, c_ref, d_ref, *outs):
    long = outs[0].shape[0]
    for i, out in enumerate(outs):
        at = slice(i * long, (i + 1) * long)
        total = a_ref[at].astype(F32) + b_ref[at].astype(F32)
        out[...] = (total + (c_ref[at].astype(F32) + d_ref[at].astype(F32))).astype(BF)


def combine_kernel(pos, picks_ref, *refs):
    out_ref = refs[-1]
    zs, rows, wide = out_ref.shape
    tokens = zs * rows
    width = wide - LANES
    slots = refs[0].shape[0] - 8
    result = jnp.zeros((tokens, width), F32)
    gates = []
    for k in range(4):
        total = refs[k][...]
        pick = picks_ref[k, :slots]
        result += lax.dot_general(pick, total[:slots], TN, preferred_element_type=F32)
        line = jnp.dot(total[slots:, :LANES], picks_ref[k], preferred_element_type=F32)
        gates.append(line[:1])
    gates = jnp.concatenate(gates + [jnp.zeros((rows - 4, tokens), F32)], axis=0).astype(BF)
    result = result.astype(BF)
    for z in range(zs):
        out_ref[z, :, :width] = result[z * rows : (z + 1) * rows]
        out_ref[z, :, width:] = gates


def gather_kernel(pos, ids_ref, got_ref, out_ref, gate_ref):
    width = out_ref.shape[2]
    total = got_ref[0].astype(F32)
    for z in range(1, got_ref.shape[0]):
        total += got_ref[z].astype(F32)
    slab = total[:, :width].astype(BF)
    for z in range(out_ref.shape[0]):
        out_ref[z] = slab
    ids = ids_ref[...]
    gates = jnp.zeros(ids.shape, F32)
    for k, offset in enumerate(OFFSETS):
        hit = ids == lax.rem(pos[1] + offset + 4, 4)
        gates += jnp.where(hit, total[k : k + 1, width:], 0.0)
    gate_ref[...] = gates.astype(BF)


def columns_kernel(pos, *refs):
    pieces, out_ref, sems = refs[:4], refs[4], refs[5]
    width = pieces[0].shape[1]
    copies = []
    for k, shift in enumerate((0, 1, -1, 2)):
        block = lax.rem(pos[3] - shift + 4 + 2 * pos[0], 4)
        at = pl.multiple_of(block * width, LANES)
        copies.append(
            pltpu.make_async_copy(pieces[k], out_ref.at[:, pl.ds(at, width)], sems.at[k])
        )
    for copy in copies:
        copy.start()
    for copy in copies:
        copy.wait()


def grad_kernel(other, pos, here_ref, far_ref, plus_ref, minus_ref, *refs):
    msgs = (here_ref, far_ref, plus_ref, minus_ref)
    auxs, added, outs = refs[:3], refs[3:-3], refs[-3:]
    half, units = outs[0].shape
    width = 2 * half
    base = ((1 - pos[0]) if other else pos[0]) * half
    step = 256
    right = jnp.concatenate([ref[:, : 2 * units] for ref in auxs], axis=0)
    hidden = jnp.concatenate([ref[:, 2 * units : 3 * units] for ref in auxs], axis=0)
    for i in range(half // step):
        rows = slice(i * step, (i + 1) * step)

        def left(start):
            at = pl.multiple_of(start + base + i * step, LANES)
            return jnp.concatenate([msg[:, pl.ds(at, step)] for msg in msgs], axis=0)

        both = lax.dot_general(left(0), right, TN, preferred_element_type=F32)
        down = lax.dot_general(left(width), hidden, TN, preferred_element_type=F32)
        for k, total in enumerate((both[:, :units], both[:, units:], down)):
            if added:
                total += added[k][rows].astype(F32)
            outs[k][rows] = total.astype(BF)


def shift(value, axis, offset):
    size = lax.axis_size(axis)
    return lax.ppermute(value, axis, [(i, (i + offset) % size) for i in range(size)])


def swap(value):
    size = lax.axis_size("z")
    return lax.ppermute(value, "z", [(i, i ^ 1) for i in range(size)])


def exchange(value, axis):
    return lax.all_to_all(value, axis, split_axis=0, concat_axis=0, tiled=True)


def after(value, *others):
    return lax.optimization_barrier((value, *others))[0]


def on_device(tokens, cotangent, gate_weights, expert_ids, w_gate, w_up, w_down):
    tok_count, width = tokens.shape
    slots = tok_count * 3 // 4
    units = w_gate.shape[2]
    block = width // 4
    zs = lax.axis_size("z")
    rows = tok_count // zs
    long = 2 * width + LANES
    pos = jnp.stack(
        [lax.axis_index(name) for name in ("dp", "expert", "z", "y")]
    ).astype(jnp.int32)
    given = (expert_ids.T, gate_weights.T)

    far, tokens, cotangent = call(
        far_kernel,
        [array(slots // 2, width + LANES), array(*tokens.shape), array(*tokens.shape)],
        (pos, *given, tokens, cotangent),
        free=(0, 1, 2, 3),
        unblocked=(0, 1, 2, 3),
        scratch=[
            pltpu.VMEM(given[0].shape, jnp.int32),
            pltpu.VMEM(given[1].shape, BF),
            pltpu.SemaphoreType.DMA((4,)),
        ],
    )
    given = (*given, tokens, cotangent)
    part = width // 4
    plus, minus, plus_part, minus_part = call(
        sides_kernel,
        [array(slots, long - 2 * part)] * 2 + [array(slots, part)] * 2,
        (pos, *given),
        free=(0, 1),
    )
    then = after(pos, plus)
    here, chosen = call(
        here_kernel, [array(slots, long), array(4, LANES, tok_count)], (then, *given), free=(0, 1)
    )
    weights = []
    for own in (w_gate, w_up, w_down):
        weights += [own, shift(after(own, plus), "dp", 1)]
    plus_part = shift(plus_part, "expert", 1)
    minus_part = shift(minus_part, "expert", -1)
    plus, minus = shift(plus, "expert", 1), shift(minus, "expert", -1)
    sides_in = [plus, minus, plus_part, minus_part, swap(plus_part), swap(minus_part)]
    far = shift(far, "expert", 2)
    far = [far] + [shift(far, "y", offset) for offset in (1, -1, 2)]

    def expert(pos, msgs, kind):
        count = 2 if kind == "sides" else 1
        return call(
            functools.partial(expert_kernel, kind),
            [array(count * (slots + 8), block)] * 4
            + [array(count * slots, 3 * units)]
            + [array(slots, long)] * {"here": 0, "far": 1, "sides": 2}[kind],
            (pos, *msgs, *weights),
            scratch=[pltpu.VMEM((4, count * slots, block), BF)],
        )

    def scatter(sends, name):
        got = [sends[0]]
        for j in (1, 3, 2):
            got.append(shift(sends[j], "y", j))
        count = 2 if name == "sides" else 1
        return call(sum_kernel, [array(slots + 8, block)] * count, (pos, *got))

    local = expert(pos, [here], "here")
    remote = expert(after(pos, local[0]), far, "far")
    sides = expert(after(pos, remote[0]), sides_in, "sides")
    (from_here,) = scatter(local[:4], "here")
    (from_far,) = scatter(remote[:4], "far")
    from_plus, from_minus = scatter(sides[:4], "sides")
    groups = [
        from_here,
        shift(from_plus, "expert", -1),
        shift(from_minus, "expert", 1),
        shift(from_far, "expert", 2),
    ]
    (mine,) = call(combine_kernel, [array(zs, rows, block + LANES)], (pos, chosen, *groups))
    mine, gate_grad = call(
        gather_kernel,
        [array(zs, rows, block), plain(2, tok_count)],
        (pos, expert_ids.T, exchange(mine, "z")),
    )
    slab = exchange(mine, "z").reshape(tok_count, block)
    (input_grad,) = call(
        columns_kernel,
        [plain(tok_count, width)],
        (pos, slab, *[shift(slab, "y", offset) for offset in (1, -1, 2)]),
        out=pl.BlockSpec(memory_space=pl.ANY),
        scratch=[pltpu.SemaphoreType.DMA((4,))],
    )
    used = [here, remote[5], sides[5], sides[6], local[4], remote[4], sides[4]]
    half = width // 2
    away = call(
        functools.partial(grad_kernel, True), [array(half, units)] * 3, (pos, *used),
        limit=12,
    )
    received = [shift(part, "dp", 1) for part in away]
    grads = call(
        functools.partial(grad_kernel, False), [plain(half, units)] * 3, (pos, *used, *received),
        limit=12,
    )
    return (input_grad, gate_grad.T, grads[0][None], grads[1][None], grads[2][None])


def solution(mesh):
    dp, experts, tensor = (mesh.shape[name] for name in ("dp", "expert", "tensor"))
    view = Mesh(mesh.devices.reshape(dp, experts, tensor // 4, 4), ("dp", "expert", "z", "y"))
    row = P(("dp", "expert"), None)
    weight = P("expert", "dp", ("z", "y"))

    return jax.shard_map(
        on_device,
        mesh=view,
        in_specs=(row, row, row, row, weight, weight, weight),
        out_specs=(row, row, weight, weight, weight),
        check_vma=False,
    )
```
